128 devices in a mesh: tensor: 16 (over y, x), dp: 8 (over z, core).
Axes of the slice: x: 4, y: 4, z: 4, core: 2. Of those that a mesh axis runs over, the one named last changes fastest.
Arguments:
- tokens: bfloat16 [12288, 6144], P('dp', 'tensor'), may hold values from -9 to 9
- expert_ids: int32 [12288, 2], P('dp'), may hold values from 0 to 7, as said below
- gate_probs: float32 [12288, 2], P('dp'), may hold values from 0.2 to 1
- gate_weight: bfloat16 [6144, 8192], P(None, 'tensor'), may hold values from -0.078125 to 0.078125
- up_weight: bfloat16 [6144, 8192], P(None, 'tensor'), may hold values from -0.078125 to 0.078125
- down_weight: bfloat16 [8192, 6144], P('tensor'), may hold values from -0.09375 to 0.09375
Outputs:
- expert_out: bfloat16 [12288, 6144], P('dp', 'tensor')
- peaks: float32 [2], replicated
The draws below stay inside these ranges and needn't reach their ends.
Inputs may be any that keep to these rules, and one draw needn't show every extreme that they name: `expert_ids`: each row names two different experts. In each aligned block of 1536 rows at most 768 rows name expert 0, and in some block exactly 768 do.
All inputs are finite; a program needn't handle non-finite values.
Results may differ from the reference program's by a relative error of at most 0.02.
Values may be sent and summed in bfloat16 or wider, within the bound.
A program may use at most 128 MiB of HBM per device.

```python
import math
import jax
import jax.numpy as jnp
from jax import lax

D = 6144
EXPERTS = 8
FF_WIN = 8192
TOP = 2
TOK_DEV = 1536
CAP = 768
TOKENS = 12288
N_TENSOR = 16


def draw_tokens(key, part):
    subkeys = jax.random.split(key, 2)
    place_in = jnp.arange(TOKENS, dtype=jnp.float32) / max(TOKENS - 1, 1)
    row_rise = 3.0 ** place_in
    roughness = jax.random.uniform(subkeys[0], (TOKENS,), jnp.float32, 0.5, 1.5)
    base_draw = jnp.clip(0.5 * jax.random.normal(subkeys[1], (TOKENS, D), jnp.float32), -2.0, 2.0)
    return (base_draw * (row_rise * roughness)[:, None]).astype(jnp.bfloat16)


def draw_expert_ids(key, part):
    blocks = TOKENS // TOK_DEV
    subkeys = jax.random.split(jax.random.fold_in(key, 17), 6)
    counts = jax.random.randint(subkeys[0], (blocks,), CAP // 2, CAP + 1)
    fullest = jax.random.randint(subkeys[1], (), 0, blocks)
    counts = jnp.where(jnp.arange(blocks) == fullest, CAP, counts)
    orders = jax.vmap(lambda sub_key: jax.random.permutation(sub_key, TOK_DEV))(jax.random.split(subkeys[2], blocks))
    rank_of = jnp.argsort(orders, axis=1, stable=True)
    chosen = (rank_of < counts[:, None]).reshape(TOKENS)
    first_pick = jax.random.randint(subkeys[3], (TOKENS,), 1, EXPERTS)
    second = 1 + (first_pick - 1 + jax.random.randint(subkeys[4], (TOKENS,), 1, EXPERTS - 1)) % (EXPERTS - 1)
    second = jnp.where(chosen, 0, second)
    swapped = jax.random.randint(subkeys[5], (TOKENS,), 0, 2) == 1
    column_a = jnp.where(swapped, second, first_pick)
    column_b = jnp.where(swapped, first_pick, second)
    return jnp.stack([column_a, column_b], axis=1).astype(jnp.int32)


def raised(result, stream_key, source, target, blocks, factor):
    owner, partner = [(jnp.arange(result.shape[dim]) // (result.shape[dim] // blocks)).reshape([-1 if axis == dim else 1 for axis in range(result.ndim)]) for dim in (source, target)]
    chosen = jax.random.permutation(stream_key, blocks)[partner]
    strong = (owner == chosen) | (owner == (partner + blocks // 2) % blocks)
    return jnp.where(strong, factor * result, result)


def block_levels(stream_key, shape, cuts, low, largest):
    factor_of, own = 1.0, jax.random.fold_in(stream_key, 6)
    for axis_at, shards_of in cuts:
        steps = jnp.exp(jax.random.uniform(jax.random.fold_in(own, axis_at), (shards_of,), jnp.float32, low / len(cuts), largest / len(cuts)))
        factor_of = factor_of * jnp.repeat(steps, shape[axis_at] // shards_of).reshape([-1 if axis == axis_at else 1 for axis in range(len(shape))])
    return factor_of


def gaussian(own_key, shape, spread, limit, pieces=(), held_as=jnp.bfloat16):
    array = spread * jax.random.normal(own_key, shape, jnp.float32)
    if pieces:
        array = array * block_levels(own_key, shape, pieces, -0.22, 0.18)
    return jnp.clip(array, -limit, limit).astype(held_as)


def noise_with(rng, dims, width, limit, shards, heavy, kind=jnp.bfloat16):
    result = width * jax.random.normal(rng, dims, jnp.float32)
    if shards:
        result = result * block_levels(rng, dims, shards, -0.22, 0.18)
    return jnp.clip(raised(result, jax.random.fold_in(rng, 3), *heavy), -limit, limit).astype(kind)


def setup_inputs(seed: int = 0) -> dict:
    streams_of = jax.random.split(jax.random.key(seed), 7)
    tokens = draw_tokens(jax.random.fold_in(streams_of[6], 71), 0)
    expert_ids = draw_expert_ids(jax.random.fold_in(streams_of[6], 71), 0)
    gate_probs = jnp.clip(0.2 + 0.8 * jax.random.uniform(streams_of[2], (TOKENS, TOP), jnp.float32) ** block_levels(streams_of[2], (TOKENS, TOP), ((0, 8),), -0.2, 0.2), 0.2, 1.0)
    gate_weight = gaussian(streams_of[3], (D, FF_WIN), D ** -0.5, 0.078125, ((1, 16),))
    up_weight = gaussian(streams_of[4], (D, FF_WIN), D ** -0.5, 0.078125, ((1, 16),))
    down_weight = noise_with(streams_of[5], (FF_WIN, D), FF_WIN ** -0.5, 0.09375, ((0, 16),), (0, 1, 16, 2.0))
    return {"tokens": tokens, "expert_ids": expert_ids, "gate_probs": gate_probs, "gate_weight": gate_weight, "up_weight": up_weight, "down_weight": down_weight}


clip_share = 0.25

def sylvester(order_size):
    index_row = jnp.arange(order_size, dtype=jnp.int32)
    common = index_row[:, None] & index_row[None, :]
    parity = jnp.zeros((order_size, order_size), jnp.int32)
    for bit_pos in range(order_size.bit_length() - 1):
        parity = parity ^ common >> bit_pos & 1
    return (1 - 2 * parity).astype(jnp.float32)

def routing(expert_ids, gate_probs, capacity):
    hits = expert_ids == 0
    routed = jnp.any(hits, axis=1)
    share_of = lax.optimization_barrier(jnp.sum(jnp.where(hits, gate_probs, 0.0), axis=1))
    position = (jnp.cumsum(routed.astype(jnp.int32)) - 1).astype(jnp.int32)
    routed_count = jnp.sum(routed.astype(jnp.int32)).astype(jnp.int32)
    target_slot = jnp.where(routed, position, capacity).astype(jnp.int32)
    row_numbers = jnp.arange(expert_ids.shape[0], dtype=jnp.int32)
    source = jnp.zeros((capacity,), jnp.int32).at[target_slot].set(row_numbers, mode='drop')
    filled = jnp.arange(capacity, dtype=jnp.int32) < routed_count
    slot_of_row = jnp.clip(position, 0, capacity - 1).astype(jnp.int32)
    return (routed, share_of, source, filled, slot_of_row)

def rotate(hidden):
    bits = FF_WIN.bit_length() - 1
    outer_size = 2 ** (bits // 2)
    inner_size = FF_WIN // outer_size
    grid = hidden.astype(jnp.float32).reshape(hidden.shape[0], outer_size, inner_size)
    first_pass = jnp.einsum('rab,bd->rad', grid, sylvester(inner_size), precision=lax.Precision.HIGHEST)
    second_pass = jnp.einsum('rad,ac->rcd', first_pass, sylvester(outer_size), precision=lax.Precision.HIGHEST)
    return second_pass.reshape(hidden.shape[0], FF_WIN) * (1.0 / math.sqrt(FF_WIN))

def reference(tokens, expert_ids, gate_probs, gate_weight, up_weight, down_weight):
    blocks = TOKENS // TOK_DEV
    routes = []
    rotations = []
    input_peaks = []
    for block_idx in range(blocks):
        lower = block_idx * TOK_DEV
        token_block = tokens[lower:lower + TOK_DEV]
        info = routing(expert_ids[lower:lower + TOK_DEV], gate_probs[lower:lower + TOK_DEV], CAP)
        routes.append(info)
        picked = jnp.where(info[3][:, None], token_block[info[2]], jnp.zeros((), tokens.dtype))
        input_peaks.append(jnp.max(jnp.abs(picked)).astype(jnp.float32))
        gate_part = jnp.dot(picked, gate_weight, preferred_element_type=jnp.float32)
        up_part = jnp.dot(picked, up_weight, preferred_element_type=jnp.float32)
        hidden = (jax.nn.silu(gate_part) * up_part).astype(jnp.bfloat16)
        rotations.append(rotate(hidden))
    peak_in = jnp.max(jnp.stack(input_peaks))
    peak_rot = jnp.max(jnp.stack([jnp.max(jnp.abs(item)) for item in rotations]))
    clip_level = clip_share * peak_rot
    group_width = FF_WIN // N_TENSOR
    outputs = []
    for block_idx in range(blocks):
        routed, share_of, source, filled, slot_of_row = routes[block_idx]
        clipped = jnp.clip(rotations[block_idx], -clip_level, clip_level).astype(jnp.bfloat16)
        summed = jnp.zeros((CAP, D), jnp.float32)
        for group in range(N_TENSOR):
            lower = group * group_width
            term = jnp.dot(clipped[:, lower:lower + group_width], down_weight[lower:lower + group_width], preferred_element_type=jnp.float32)
            rounded = lax.optimization_barrier(term.astype(jnp.bfloat16))
            summed = summed + rounded.astype(jnp.float32)
        block_out = jnp.where(routed[:, None], share_of[:, None] * summed[slot_of_row], 0.0)
        outputs.append(block_out.astype(jnp.bfloat16))
    return (jnp.concatenate(outputs, axis=0), jnp.stack([peak_in, peak_rot]))
```

```python
import jax
import jax.numpy as jnp
from jax import lax
from jax.experimental import pallas as pl
from jax.experimental.pallas import tpu as pltpu
from jax.sharding import Mesh
from jax.sharding import PartitionSpec as P

CAP = 768
TOK = 1536
D = 6144
SL = 384
HID = 512
NCH = 3
CH = CAP // NCH
HALF = ((0, 128), (128, 128))
Y, X, Z, C = "tensor_0", "tensor_1", "dp_0", "dp_1"
TENSOR = (Y, X)
DP = (Z, C)
MESH = pl.DeviceIdType.MESH
clip_share = 0.25
BF, F32 = jnp.bfloat16, jnp.float32


def body(
    slot_row, share_row, slot_col, tok, h128, wg, wu, wd,
    out, peaks,
    xb, wgu, wd2, acc, hid, a1, rin, rout, cl, clp, s1, r1, pf, of, s2, r2, shs, pks, pkr, pkm,
    ag_r, ag_s, a1_r, a1_s, r_r, r_s, q_r, q_s, g_r, g_s, t_r, t_s,
    w1_r, w1_s, w2_r, w2_s, w3_r, w3_s, pk_r, pk_s, loc,
):
    y, x, z, c_ = (lax.axis_index(a) for a in (Y, X, Z, C))
    pos = {Y: y, X: x, Z: z, C: c_}
    size = {Y: 4, X: 4, Z: 4, C: 2}

    def nb(axis, d):
        return lax.rem(pos[axis] + (d % size[axis]), size[axis])

    def rcopy(src, dst, ss, rs, axis, d):
        return pltpu.make_async_remote_copy(
            src_ref=src, dst_ref=dst, send_sem=ss, recv_sem=rs,
            device_id={axis: nb(axis, d)}, device_id_type=MESH)

    def send(src, dst, ss, rs, axis, d):
        rcopy(src, dst, ss, rs, axis, d).start()

    def wait_r(ref, sem):
        rcopy(ref, ref, ag_s.at[0, 0], sem, X, 1).wait_recv()

    def wait_s(ref, sem):
        rcopy(ref, ref, sem, ag_r.at[0, 0, 0], X, 1).wait_send()

    def load_w():
        for n in range(2):
            pltpu.make_async_copy(wg.at[:, pl.ds(n * 256, 256)], wgu.at[n], loc.at[n]).start()
            pltpu.make_async_copy(wu.at[:, pl.ds(n * 256, 256)], wgu.at[2 + n], loc.at[2 + n]).start()

    def strip(yy, xx):
        return pl.ds(pl.multiple_of((yy * 4 + xx) * SL, 128), SL)

    def own_wd(start):
        for yy in range(4):
            k = pltpu.make_async_copy(
                wd.at[:, strip(yy, x)],
                wd2.at[yy, pl.ds(pl.multiple_of(x * HID, HID), HID), :], loc.at[4 + yy])
            k.start() if start else k.wait()

    load_w()
    own_wd(True)

    barrier = pltpu.get_barrier_semaphore()
    for axis in (Y, X, Z, C):
        for d in range(1, size[axis]):
            pl.semaphore_signal(barrier, inc=1, device_id={axis: nb(axis, d)}, device_id_type=MESH)
    pl.semaphore_wait(barrier, 10)

    me = y * 4 + x

    def pick(c):
        ids = lax.broadcasted_iota(jnp.int32, (CH, TOK), 0) + c * CH
        hit = ids == slot_row[...]
        one = jnp.where(hit, 1.0, 0.0).astype(BF)
        rows = jnp.dot(one, tok[...], preferred_element_type=F32)
        xb[me, pl.ds(c * CH, CH), :] = rows.astype(BF)
        shs[pl.ds(c * CH, CH), :] = jnp.sum(jnp.where(hit, share_row[...], 0.0), axis=1, keepdims=True)
        m = jnp.max(jnp.max(jnp.abs(rows), axis=0, keepdims=True), axis=1, keepdims=True)
        pkm[pl.ds(0, 1), :] = jnp.maximum(pkm[pl.ds(0, 1), :], m) if c else jnp.broadcast_to(m, (1, 128))

    AX = ((X, Y), (Y, X))

    def rows_of(c, h):
        o, n = HALF[h]
        return pl.ds(c * CH + o, n)

    def sid(h, ka, kb):
        a, b = AX[h]
        pa, pb = lax.rem(pos[a] + (ka % 4), 4), lax.rem(pos[b] + (kb % 4), 4)
        return pb * 4 + pa if h == 0 else pa * 4 + pb

    def piece(c, h, ka, kb):
        return xb.at[sid(h, ka, kb), rows_of(c, h)]

    def ag_send(c, h, ka, kb, which, d, idx):
        p = piece(c, h, ka, kb)
        send(p, p, ag_s.at[c, h], ag_r.at[c, h, idx], AX[h][which], d)

    def ag_wait(c, h, ka, kb, idx):
        wait_r(piece(c, h, ka, kb), ag_r.at[c, h, idx])

    def line(c, h, k):
        ag_send(c, h, k, 0, 1, 1, 3 + 3 * k)
        ag_send(c, h, k, 0, 1, -1, 4 + 3 * k)

    def ag1(c):
        for h in range(2):
            ag_send(c, h, 0, 0, 0, 1, 0)
            ag_send(c, h, 0, 0, 0, -1, 1)
        for h in range(2):
            line(c, h, 0)

    def agf1(c):
        for h in range(2):
            fwd = (c + h) % 2 == 0
            ag_wait(c, h, -1, 0, 0)
            if fwd:
                ag_send(c, h, -1, 0, 0, 1, 2)
            line(c, h, 3)
            ag_wait(c, h, 1, 0, 1)
            if not fwd:
                ag_send(c, h, 1, 0, 0, -1, 2)
            line(c, h, 1)

    def agf1b(c):
        for h in range(2):
            ag_wait(c, h, 2, 0, 2)
            line(c, h, 2)

    def agf2(c, k):
        for h in range(2):
            ag_wait(c, h, k, -1, 3 + 3 * k)
            if k % 2 == 0:
                ag_send(c, h, k, -1, 1, 1, 5 + 3 * k)
            ag_wait(c, h, k, 1, 4 + 3 * k)
            if k % 2 == 1:
                ag_send(c, h, k, 1, 1, -1, 5 + 3 * k)

    def agw(c):
        for h in range(2):
            for k in range(4):
                ag_wait(c, h, k, 2, 5 + 3 * k)

    def gu(c, sy):
        if c == 0 and sy == 0:
            for n in range(2):
                pltpu.make_async_copy(wg.at[:, pl.ds(n * 256, 256)], wgu.at[n], loc.at[n]).wait()
                pltpu.make_async_copy(wu.at[:, pl.ds(n * 256, 256)], wgu.at[2 + n], loc.at[2 + n]).wait()

        @pl.loop(0, 4)
        def _(n):
            lhs = jnp.concatenate([xb[sy * 4 + sx, pl.ds(c * CH, CH), :] for sx in range(4)], axis=1)
            r = jnp.dot(lhs, wgu[n, pl.ds(sy * 1536, 1536), :], preferred_element_type=F32)
            acc[n] = r if sy == 0 else acc[n] + r

    def act(c):
        for n in range(2):
            g = acc[n]
            hid[c, :, pl.ds(n * 256, 256)] = (g / (1.0 + jnp.exp(-g)) * acc[2 + n]).astype(BF)
        mycol = pl.ds(pl.multiple_of(x * HID, HID), HID)
        for d in (1, -1, 2):
            send(hid.at[c, pl.ds(pl.multiple_of(nb(X, d) * 64, 64), 64), :], a1.at[c, :, mycol],
                 a1_s.at[c], a1_r.at[c, d % 4 - 1], X, d)
        a1[c, :, mycol] = hid[c, pl.ds(pl.multiple_of(x * 64, 64), 64), :]

    def a2a_y(c):
        for d in (1, -1, 2):
            wait_r(a1.at[c, :, pl.ds(pl.multiple_of(nb(X, -d) * HID, HID), HID)], a1_r.at[c, d % 4 - 1])
        mycol = pl.ds(pl.multiple_of(y * 2048, 2048), 2048)
        for d in (1, -1, 2):
            send(a1.at[c, pl.ds(pl.multiple_of(nb(Y, d) * 16, 16), 16), :], rin.at[c, :, mycol],
                 r_s.at[c], r_r.at[c, d % 4 - 1], Y, d)
        rin[c, :, mycol] = a1[c, pl.ds(pl.multiple_of(y * 16, 16), 16), :]

    def rotate(c):
        for d in (1, -1, 2):
            wait_r(rin.at[c, :, pl.ds(pl.multiple_of(nb(Y, -d) * 2048, 2048), 2048)], r_r.at[c, d % 4 - 1])
        v = jnp.concatenate([rin[c, :, pl.ds(a * 128, 128)] for a in range(64)], axis=0)
        v = jnp.dot(v, h128[...], preferred_element_type=F32)
        for s in range(6):
            w = 16 << s
            v = v.reshape(1024 // (2 * w), 2, w, 128)
            p, q = v[:, 0:1], v[:, 1:2]
            v = jnp.concatenate([p + q, p - q], axis=1)
        v = v.reshape(1024, 128) * (1.0 / 8192.0 ** 0.5)
        m = jnp.max(jnp.max(jnp.abs(v), axis=0, keepdims=True), axis=1, keepdims=True)
        pkm[pl.ds(1, 1), :] = jnp.maximum(pkm[pl.ds(1, 1), :], m) if c else jnp.broadcast_to(m, (1, 128))
        v = v.astype(BF)
        for a in range(64):
            rout[c, :, pl.ds(a * 128, 128)] = v[a * 16:(a + 1) * 16]

    def back_y(c):
        myrow = pl.ds(pl.multiple_of(y * 16, 16), 16)
        for d in (1, -1, 2):
            send(rout.at[c, :, pl.ds(pl.multiple_of(nb(Y, d) * 2048, 2048), 2048)], cl.at[c, x, myrow, :],
                 q_s.at[c], q_r.at[c, d % 4 - 1], Y, d)
        cl[c, x, myrow, :] = rout[c, :, pl.ds(pl.multiple_of(y * 2048, 2048), 2048)]

    def back_x(c):
        for d in (1, -1, 2):
            wait_r(cl.at[c, x, pl.ds(pl.multiple_of(nb(Y, -d) * 16, 16), 16), :], q_r.at[c, d % 4 - 1])
        p = cl.at[c, x]
        send(p, p, g_s.at[c], g_r.at[c, 0], X, 1)
        send(p, p, g_s.at[c], g_r.at[c, 1], X, -1)

    def back_f(c):
        wait_r(cl.at[c, nb(X, -1)], g_r.at[c, 0])
        p = cl.at[c, nb(X, -1), pl.ds(0, 32), :]
        send(p, p, g_s.at[c], g_r.at[c, 2], X, 1)
        wait_r(cl.at[c, nb(X, 1)], g_r.at[c, 1])
        p = cl.at[c, nb(X, 1), pl.ds(32, 32), :]
        send(p, p, g_s.at[c], g_r.at[c, 3], X, -1)

    def back_w(c):
        wait_r(cl.at[c, nb(X, 2), pl.ds(0, 32), :], g_r.at[c, 2])
        wait_r(cl.at[c, nb(X, 2), pl.ds(32, 32), :], g_r.at[c, 3])

    e = c_ * 4 + z

    def w_1():
        src_rows = pl.ds(pl.multiple_of(e * 64, 64), 64)
        for d in (1, -1, 2):
            for yy in range(4):
                send(wd.at[src_rows, strip(yy, nb(X, d))],
                     wd2.at[yy, pl.ds(pl.multiple_of(x * HID + e * 64, 64), 64), :],
                     w1_s.at[d % 4 - 1], w1_r.at[d % 4 - 1], X, d)

    def w_rows(g, ee, n):
        return wd2.at[:, pl.ds(pl.multiple_of(g * HID + ee * 64, 64), n), :]

    def w_2():
        for d in (1, -1, 2):
            wait_r(w_rows(nb(X, -d), e, 64), w1_r.at[d % 4 - 1])
        for dz in (1, -1, 2):
            for d in (1, -1, 2):
                p = w_rows(nb(X, d), e, 64)
                send(p, p, w2_s.at[d % 4 - 1], w2_r.at[dz % 4 - 1, d % 4 - 1], Z, dz)

    def w_3():
        for dz in (1, -1, 2):
            for d in (1, -1, 2):
                wait_r(w_rows(nb(X, d), c_ * 4 + nb(Z, -dz), 64), w2_r.at[dz % 4 - 1, d % 4 - 1])
        for d in (1, -1, 2):
            p = w_rows(nb(X, d), c_ * 4, 256)
            send(p, p, w3_s.at[d % 4 - 1], w3_r.at[d % 4 - 1], C, 1)

    def w_4():
        for d in (1, -1, 2):
            wait_r(w_rows(nb(X, d), (1 - c_) * 4, 256), w3_r.at[d % 4 - 1])
        own_wd(False)

    def pk_send(i, axis):
        if i == 0:
            pks[0] = pkm[...]
        for d in range(1, size[axis]):
            send(pks.at[i], pkr.at[i, d - 1], pk_s.at[i, d - 1], pk_r.at[i, d - 1], axis, d)

    def pk_wait(i, axis):
        v = pks[i]
        for d in range(1, size[axis]):
            wait_r(pkr.at[i, d - 1], pk_r.at[i, d - 1])
            v = jnp.maximum(v, pkr[i, d - 1])
        pks[i + 1] = v

    lo, hi = pl.ds(0, 128), pl.ds(128, 128)

    def down(c):
        lim = (clip_share * pks[4, pl.ds(1, 1), pl.ds(0, 1)]).astype(BF)
        for xs in range(4):
            clp[pl.ds(xs * 64, 64), :] = jnp.minimum(jnp.maximum(cl[c, xs], -lim), lim)

        def part(d):
            return jnp.dot(clp[...], wd2[nb(Y, d)], preferred_element_type=F32)

        s1[c] = part(2).astype(BF)
        send(s1.at[c, lo, :], r1.at[c, lo, :], t_s.at[c, 0], t_r.at[c, 0], Y, -1)
        send(s1.at[c, hi, :], r1.at[c, hi, :], t_s.at[c, 0], t_r.at[c, 1], Y, 1)
        pf[c, 0] = part(-1)
        pf[c, 1] = part(1)
        of[c] = part(0)

    def down2(c):
        wait_r(r1.at[c, lo, :], t_r.at[c, 0])
        s2[c, 0, lo, :] = (pf[c, 0, lo, :] + r1[c, lo, :].astype(F32)).astype(BF)
        s2[c, 0, hi, :] = pf[c, 0, hi, :].astype(BF)
        send(s2.at[c, 0], r2.at[c, 0], t_s.at[c, 1], t_r.at[c, 2], Y, -1)
        wait_r(r1.at[c, hi, :], t_r.at[c, 1])
        s2[c, 1, lo, :] = pf[c, 1, lo, :].astype(BF)
        s2[c, 1, hi, :] = (pf[c, 1, hi, :] + r1[c, hi, :].astype(F32)).astype(BF)
        send(s2.at[c, 1], r2.at[c, 1], t_s.at[c, 1], t_r.at[c, 3], Y, 1)

    def finish(c):
        wait_r(r2.at[c, 0], t_r.at[c, 2])
        wait_r(r2.at[c, 1], t_r.at[c, 3])
        tot = of[c] + r2[c, 0].astype(F32) + r2[c, 1].astype(F32)
        sc = (tot * shs[pl.ds(c * CH, CH), :]).astype(BF)

        @pl.loop(0, TOK, step=256)
        def _(o):
            o = pl.multiple_of(o, 256)
            ids = lax.broadcasted_iota(jnp.int32, (256, CH), 1) + c * CH
            one = jnp.where(ids == slot_col[pl.ds(o, 256), :], 1.0, 0.0).astype(BF)
            r = jnp.dot(one, sc, preferred_element_type=F32).astype(BF)
            out[pl.ds(o, 256), :] = out[pl.ds(o, 256), :] + r if c else r

    pkm[...] = jnp.zeros_like(pkm)
    pick(0)
    ag1(0)
    pick(1)
    agf1(0)
    w_1()
    ag1(1)
    pick(2)
    agf1b(0)
    agf2(0, 0)
    agf2(0, 3)
    agf1(1)
    agf2(0, 1)
    agf2(0, 2)
    agf1b(1)
    ag1(2)
    agw(0)
    w_2()
    gu(0, 0)
    agf2(1, 0)
    gu(0, 1)
    agf2(1, 3)
    agf1(2)
    gu(0, 2)
    agf2(1, 1)
    gu(0, 3)
    agf2(1, 2)
    act(0)
    agf1b(2)
    agw(1)
    gu(1, 0)
    agf2(2, 0)
    gu(1, 1)
    agf2(2, 3)
    a2a_y(0)
    gu(1, 2)
    agf2(2, 1)
    gu(1, 3)
    agf2(2, 2)
    act(1)
    rotate(0)
    back_y(0)
    agw(2)
    for sy in range(4):
        gu(2, sy)
    act(2)
    a2a_y(1)
    back_x(0)
    rotate(1)
    back_y(1)
    a2a_y(2)
    back_f(0)
    rotate(2)
    pk_send(0, X)
    back_y(2)
    back_x(1)
    pk_wait(0, X)
    pk_send(1, Y)
    back_x(2)
    w_3()
    back_f(1)
    pk_wait(1, Y)
    pk_send(2, Z)
    back_w(0)
    pk_wait(2, Z)
    pk_send(3, C)
    back_f(2)
    w_4()
    pk_wait(3, C)
    peaks[...] = pks[4]
    down(0)
    back_w(1)
    down(1)
    down2(0)
    back_w(2)
    down(2)
    down2(1)
    down2(2)
    for c in range(NCH):
        finish(c)

    for c in range(NCH):
        for h in range(2):
            wait_s(xb.at[pl.ds(0, 15), rows_of(c, h)], ag_s.at[c, h])
        wait_s(hid.at[c, pl.ds(0, 192), :], a1_s.at[c])
        wait_s(a1.at[c, pl.ds(0, 48), :], r_s.at[c])
        wait_s(rout.at[c, :, pl.ds(0, 6144)], q_s.at[c])
        wait_s(cl.at[c, pl.ds(0, 3)], g_s.at[c])
        wait_s(s1.at[c], t_s.at[c, 0])
        wait_s(s2.at[c], t_s.at[c, 1])
    for d in range(3):
        wait_s(w_rows(0, 0, 64), w1_s.at[d])
        wait_s(w_rows(0, 0, 192), w2_s.at[d])
        wait_s(w_rows(0, 0, 256), w3_s.at[d])
    for i, axis in enumerate((X, Y, Z, C)):
        for d in range(1, size[axis]):
            wait_s(pks.at[i], pk_s.at[i, d - 1])


def hadamard(n):
    i = jnp.arange(n, dtype=jnp.int32)
    v = i[:, None] & i[None, :]
    p = jnp.zeros_like(v)
    for b in range(n.bit_length() - 1):
        p = p ^ (v >> b & 1)
    return (1 - 2 * p).astype(BF)


def on_device(tokens, expert_ids, gate_probs, gate_weight, up_weight, down_weight):
    hits = expert_ids == 0
    routed = jnp.any(hits, axis=1)
    share = jnp.sum(jnp.where(hits, gate_probs, 0.0), axis=1)
    slot = jnp.where(routed, jnp.cumsum(routed.astype(jnp.int32)) - 1, -1)
    vm, anyspace = pl.BlockSpec(memory_space=pltpu.VMEM), pl.BlockSpec(memory_space=pl.ANY)
    V, DMA = pltpu.VMEM, pltpu.SemaphoreType.DMA
    out, peaks = pl.pallas_call(
        body,
        name="expert",
        out_shape=(jax.ShapeDtypeStruct((TOK, SL), BF), jax.ShapeDtypeStruct((8, 128), F32)),
        in_specs=[vm] * 5 + [anyspace] * 3,
        out_specs=(vm, vm),
        scratch_shapes=[
            V((16, CAP, SL), BF),
            V((4, D, 256), BF),
            V((4, 2048, SL), BF),
            V((4, CH, 256), F32),
            V((NCH, CH, HID), BF),
            V((NCH, 64, 2048), BF),
            V((NCH, 16, 8192), BF),
            V((NCH, 16, 8192), BF),
            V((NCH, 4, 64, 2048), BF),
            V((CH, 2048), BF),
            V((NCH, CH, SL), BF),
            V((NCH, CH, SL), BF),
            V((NCH, 2, CH, SL), F32),
            V((NCH, CH, SL), F32),
            V((NCH, 2, CH, SL), BF),
            V((NCH, 2, CH, SL), BF),
            V((CAP, 1), F32),
            V((5, 8, 128), F32),
            V((4, 3, 8, 128), F32),
            V((8, 128), F32),
            DMA((NCH, 2, 15)), DMA((NCH, 2)),
            DMA((NCH, 3)), DMA((NCH,)),
            DMA((NCH, 3)), DMA((NCH,)),
            DMA((NCH, 3)), DMA((NCH,)),
            DMA((NCH, 4)), DMA((NCH,)),
            DMA((NCH, 4)), DMA((NCH, 2)),
            DMA((3,)), DMA((3,)),
            DMA((3, 3)), DMA((3,)),
            DMA((3,)), DMA((3,)),
            DMA((4, 3)), DMA((4, 3)),
            DMA((8,)),
        ],
        compiler_params=pltpu.CompilerParams(
            collective_id=0, has_side_effects=True, vmem_limit_bytes=66_000_000),
    )(slot[None, :], share[None, :], slot[:, None], tokens, hadamard(128), gate_weight, up_weight, down_weight)
    return out, peaks[:2, 0]


def solution(mesh):
    split = Mesh(mesh.devices.reshape(4, 4, 4, 2), (Y, X, Z, C))
    return jax.shard_map(
        on_device,
        mesh=split,
        in_specs=(P(DP, TENSOR), P(DP, None), P(DP, None), P(None, TENSOR), P(None, TENSOR), P(TENSOR, None)),
        out_specs=(P(DP, TENSOR), P()),
        check_vma=False,
    )
```

```python
import jax
import jax.numpy as jnp
from jax import lax
from jax.experimental import pallas as pl
from jax.experimental.pallas import tpu as pltpu
from jax.sharding import Mesh
from jax.sharding import PartitionSpec as P

CAP = 768
TOK = 1536
D = 6144
SL = 384
HID = 512
NCH = 3
CH = CAP // NCH
Y, X, Z, C = "tensor_0", "tensor_1", "dp_0", "dp_1"
TENSOR = (Y, X)
DP = (Z, C)
MESH = pl.DeviceIdType.MESH
clip_share = 0.25
BF, F32 = jnp.bfloat16, jnp.float32
PLANE = [(du, dv) for du in (1, -1, 2, 0) for dv in (1, -1, 2, 0) if du or dv]
DEPTH = [(dz, dc) for dz in (0, 1, -1, 2) for dc in (0, 1) if dz or dc]


def body(
    slot_row, share_row, slot_col, tok, h128, wg, wu, wd,
    out, peaks,
    xb, wgu, wd2, acc, hid, rin, rout, cl, clp, s1, r1, pf, of, s2, r2, shs, pks, pkr, pkm,
    ag_r, ag_s, a_r, a_s, q_r, q_s, g_r, g_s, t_r, t_s, w1_r, w1_s, w2_r, w2_s, pk_r, pk_s, loc,
):
    y, x, z, c_ = (lax.axis_index(a) for a in (Y, X, Z, C))
    n_ = 1 - c_
    u, v = x * n_ + y * c_, y * n_ + x * c_

    def pu(d):
        return lax.rem(u + (d + 4), 4)

    def pv(d):
        return lax.rem(v + (d + 4), 4)

    def at_uv(du, dv):
        return {Y: lax.rem(y + (du * c_ + dv * n_) + 4, 4), X: lax.rem(x + (du * n_ + dv * c_) + 4, 4)}

    def at_zc(dz, dc):
        return {Z: lax.rem(z + (dz + 4), 4), C: lax.rem(c_ + dc, 2)}

    def rcopy(src, dst, ss, rs, to):
        return pltpu.make_async_remote_copy(
            src_ref=src, dst_ref=dst, send_sem=ss, recv_sem=rs, device_id=to, device_id_type=MESH)

    def send(src, dst, ss, rs, to):
        rcopy(src, dst, ss, rs, to).start()

    def wait_s(ref, sem):
        rcopy(ref, ref, sem, pk_r.at[0], at_uv(1, 0)).wait_send()

    seen = set()

    def need(key, ref, sem):
        if key not in seen:
            seen.add(key)
            rcopy(ref, ref, pk_s.at[0], sem, at_uv(1, 0)).wait_recv()

    def mul(i, n):
        return pl.ds(pl.multiple_of(i * n, n), n)

    def tid(uu, vv):
        return (vv * 4 + uu) * n_ + (uu * 4 + vv) * c_

    def own_wd(start):
        for vv in range(4):
            k = pltpu.make_async_copy(wd.at[:, mul(tid(u, vv), SL)], wd2.at[vv, mul(u, HID), :], loc.at[4 + vv])
            k.start() if start else k.wait()

    def load():
        @pl.loop(0, 16)
        def _(s):
            src, dst = mul(tid(lax.rem(s, 4), s // 4), SL), mul(s, SL)
            for n in range(2):
                pltpu.make_async_copy(wg.at[src, pl.ds(n * 256, 256)], wgu.at[n, dst, :], loc.at[n]).start()
                pltpu.make_async_copy(wu.at[src, pl.ds(n * 256, 256)], wgu.at[2 + n, dst, :], loc.at[2 + n]).start()

        own_wd(True)

    me = v * 4 + u

    def pick(c):
        ids = lax.broadcasted_iota(jnp.int32, (CH, TOK), 0) + c * CH
        hit = ids == slot_row[...]
        one = jnp.where(hit, 1.0, 0.0).astype(BF)
        rows = jnp.dot(one, tok[...], preferred_element_type=F32)
        xb[me, pl.ds(c * CH, CH), :] = rows.astype(BF)
        shs[pl.ds(c * CH, CH), :] = jnp.sum(jnp.where(hit, share_row[...], 0.0), axis=1, keepdims=True)
        m = jnp.max(jnp.max(jnp.abs(rows), axis=0, keepdims=True), axis=1, keepdims=True)
        pkm[pl.ds(0, 1), :] = jnp.maximum(pkm[pl.ds(0, 1), :], m)

    def rows_of(c, h):
        return pl.ds(c * CH + h * 128, 128)

    def piece(c, h, ka, kb):
        du, dv = (ka, kb) if h == 0 else (kb, ka)
        return xb.at[pv(dv) * 4 + pu(du), rows_of(c, h)]

    def ag_send(c, h, ka, kb, second, d, idx):
        p = piece(c, h, ka, kb)
        along_u = (h == 0) != second
        send(p, p, ag_s.at[c, h], ag_r.at[c, h, idx], at_uv(d, 0) if along_u else at_uv(0, d))

    def ag_need(c, h, idx):
        if idx < 3:
            ka, kb = (-1, 1, 2)[idx], 0
        else:
            ka, kb = (idx - 3) // 3, (-1, 1, 2)[(idx - 3) % 3]
        need(("ag", c, h, idx), piece(c, h, ka, kb), ag_r.at[c, h, idx])

    def line(c, h, k):
        ag_send(c, h, k, 0, True, 1, 3 + 3 * k)
        ag_send(c, h, k, 0, True, -1, 4 + 3 * k)

    def own(c, h):
        ag_send(c, h, 0, 0, False, 1, 0)
        ag_send(c, h, 0, 0, False, -1, 1)
        line(c, h, 0)

    def r(c, h, k):
        forward = (c + h) % 2 == 0
        ag_need(c, h, {3: 0, 1: 1, 2: 2}[k])
        if k == 3 and forward:
            ag_send(c, h, -1, 0, False, 1, 2)
        if k == 1 and not forward:
            ag_send(c, h, 1, 0, False, -1, 2)
        line(c, h, k)

    def f(c, h, k):
        if k % 2 == 0:
            ag_need(c, h, 3 + 3 * k)
            ag_send(c, h, k, -1, True, 1, 5 + 3 * k)
        else:
            ag_need(c, h, 4 + 3 * k)
            ag_send(c, h, k, 1, True, -1, 5 + 3 * k)

    started = set()

    def gu(c, dv):
        if dv == 0:
            idxs = [(0, i) for i in (0, 1, 2)] + [(1, i) for i in (3, 4, 5)]
        else:
            e = {1: 1, 3: 0, 2: 2}[dv]
            idxs = [(0, 3 + 3 * k + e) for k in range(4)] + [(1, e)] + [(1, 3 + 3 * dv + i) for i in range(3)]
        for h, i in idxs:
            ag_need(c, h, i)
        if not started:
            for n in range(4):
                pltpu.make_async_copy(wg.at[:, pl.ds(0, 256)], wgu.at[n], loc.at[n]).wait()
        first = c not in started
        started.add(c)
        vv = pv(dv)

        @pl.loop(0, 4)
        def _(n):
            lhs = jnp.concatenate([xb[vv * 4 + uu, pl.ds(c * CH, CH), :] for uu in range(4)], axis=1)
            t = jnp.dot(lhs, wgu[n, mul(vv, 1536), :], preferred_element_type=F32)
            acc[c, n] = t if first else acc[c, n] + t

    def act(c):
        for n in range(2):
            g = acc[c, n]
            hid[c, :, pl.ds(n * 256, 256)] = (g / (1.0 + jnp.exp(-g)) * acc[c, 2 + n]).astype(BF)
        for du, dv in PLANE:
            send(hid.at[c, mul(pu(du) * 4 + pv(dv), 16), :], rin.at[c, :, mul(me, HID)],
                 a_s.at[c], a_r.at[c], at_uv(du, dv))
        rin[c, :, mul(me, HID)] = hid[c, mul(u * 4 + v, 16), :]

    def rot(c):
        need(("a", c), rin.at[c, :, pl.ds(0, 15 * HID)], a_r.at[c])
        w = jnp.concatenate([rin[c, :, pl.ds(a * 128, 128)] for a in range(64)], axis=0)
        w = jnp.dot(w, h128[...], preferred_element_type=F32)
        for s in range(6):
            n = 16 << s
            w = w.reshape(1024 // (2 * n), 2, n, 128)
            p, q = w[:, 0:1], w[:, 1:2]
            w = jnp.concatenate([p + q, p - q], axis=1)
        w = w.reshape(1024, 128) * (1.0 / 8192.0 ** 0.5)
        m = jnp.max(jnp.max(jnp.abs(w), axis=0, keepdims=True), axis=1, keepdims=True)
        pkm[pl.ds(1, 1), :] = jnp.maximum(pkm[pl.ds(1, 1), :], m)
        w = w.astype(BF)
        for a in range(64):
            rout[c, :, pl.ds(a * 128, 128)] = w[a * 16:(a + 1) * 16]

    def by(c):
        for d in (1, -1, 2):
            send(rout.at[c, :, mul(pv(d), 2048)], cl.at[c, u, mul(v, 16), :],
                 q_s.at[c], q_r.at[c, d % 4 - 1], at_uv(0, d))
        cl[c, u, mul(v, 16), :] = rout[c, :, mul(v, 2048)]

    lo32, hi32 = pl.ds(0, 32), pl.ds(32, 32)

    def by_need(c):
        for d in (1, -1, 2):
            need(("q", c, d), cl.at[c, u, mul(pv(-d), 16), :], q_r.at[c, d % 4 - 1])

    def bx(c):
        by_need(c)
        for part, d, i in ((lo32, 1, 0), (hi32, -1, 3), (hi32, 1, 1), (lo32, -1, 2)):
            p = cl.at[c, u, part, :]
            send(p, p, g_s.at[c], g_r.at[c, i], at_uv(d, 0))

    def bf(c, d):
        if d == -1:
            p = cl.at[c, pu(-1), lo32, :]
            need(("g", c, 0), p, g_r.at[c, 0])
            send(p, p, g_s.at[c], g_r.at[c, 4], at_uv(1, 0))
        else:
            p = cl.at[c, pu(1), hi32, :]
            need(("g", c, 3), p, g_r.at[c, 3])
            send(p, p, g_s.at[c], g_r.at[c, 5], at_uv(-1, 0))

    def clip(c):
        by_need(c)
        for i, (k, part) in enumerate(((-1, lo32), (-1, hi32), (1, lo32), (1, hi32), (2, lo32), (2, hi32))):
            need(("g", c, i), cl.at[c, pu(k), part, :], g_r.at[c, i])
        lim = (clip_share * pks[2, pl.ds(1, 1), pl.ds(0, 1)]).astype(BF)
        for uu in range(4):
            clp[c, pl.ds(uu * 64, 64), :] = jnp.minimum(jnp.maximum(cl[c, uu], -lim), lim)

    def w_rows(g, zz):
        return wd2.at[:, pl.ds(pl.multiple_of(g * HID + zz * 128, 128), 128), :]

    def w1():
        for d in (1, -1, 2):
            for vv in range(4):
                send(wd.at[mul(z, 128), mul(tid(pu(d), vv), SL)],
                     wd2.at[vv, pl.ds(pl.multiple_of(u * HID + z * 128, 128), 128), :],
                     w1_s.at[d % 4 - 1], w1_r.at[d % 4 - 1], at_uv(d, 0))

    def w2():
        for d in (1, -1, 2):
            need(("w1", d), w_rows(pu(-d), z), w1_r.at[d % 4 - 1])
        for dz in (1, -1, 2):
            for d in (1, -1, 2):
                p = w_rows(pu(d), z)
                send(p, p, w2_s.at[d % 4 - 1], w2_r.at[dz % 4 - 1, d % 4 - 1], at_zc(dz, 0))

    STAGES = ((DEPTH, at_zc), (PLANE, at_uv))

    def pks_(i):
        if i == 0:
            pks[0] = pkm[...]
        for j, to in enumerate(STAGES[i][0]):
            send(pks.at[i], pkr.at[i, j], pk_s.at[i], pk_r.at[i], STAGES[i][1](*to))

    def pkw(i):
        n = len(STAGES[i][0])
        need(("pk", i), pkr.at[i, pl.ds(0, n)], pk_r.at[i])
        pks[i + 1] = jnp.maximum(pks[i], jnp.max(pkr[i, pl.ds(0, n)], axis=0))
        if i == 1:
            peaks[...] = pks[2]

    lo, hi = pl.ds(0, 128), pl.ds(128, 128)

    def d(c, k):
        for dz in (1, -1, 2):
            for j in (1, -1, 2):
                need(("w2", dz, j), w_rows(pu(j), lax.rem(z - dz + 4, 4)), w2_r.at[dz % 4 - 1, j % 4 - 1])
        if "wd" not in seen:
            seen.add("wd")
            own_wd(False)
        t = jnp.dot(clp[c], wd2[pv(k)], preferred_element_type=F32)
        if k == 2:
            s1[c] = t.astype(BF)
            send(s1.at[c, lo, :], r1.at[c, lo, :], t_s.at[c, 0], t_r.at[c, 0], at_uv(0, -1))
            send(s1.at[c, hi, :], r1.at[c, hi, :], t_s.at[c, 0], t_r.at[c, 1], at_uv(0, 1))
        elif k == 0:
            of[c] = t
        else:
            pf[c, (k + 1) // 2] = t

    def s(c, k):
        if k == -1:
            need(("t", c, 0), r1.at[c, lo, :], t_r.at[c, 0])
            s2[c, 0, lo, :] = (pf[c, 0, lo, :] + r1[c, lo, :].astype(F32)).astype(BF)
            s2[c, 0, hi, :] = pf[c, 0, hi, :].astype(BF)
            send(s2.at[c, 0], r2.at[c, 0], t_s.at[c, 1], t_r.at[c, 2], at_uv(0, -1))
        else:
            need(("t", c, 1), r1.at[c, hi, :], t_r.at[c, 1])
            s2[c, 1, lo, :] = pf[c, 1, lo, :].astype(BF)
            s2[c, 1, hi, :] = (pf[c, 1, hi, :] + r1[c, hi, :].astype(F32)).astype(BF)
            send(s2.at[c, 1], r2.at[c, 1], t_s.at[c, 1], t_r.at[c, 3], at_uv(0, 1))

    done = set()

    def fin(c):
        need(("t", c, 2), r2.at[c, 0], t_r.at[c, 2])
        need(("t", c, 3), r2.at[c, 1], t_r.at[c, 3])
        tot = of[c] + r2[c, 0].astype(F32) + r2[c, 1].astype(F32)
        sc = (tot * shs[pl.ds(c * CH, CH), :]).astype(BF)
        first = not done
        done.add(c)

        @pl.loop(0, TOK, step=256)
        def _(o):
            o = pl.multiple_of(o, 256)
            ids = lax.broadcasted_iota(jnp.int32, (256, CH), 1) + c * CH
            one = jnp.where(ids == slot_col[pl.ds(o, 256), :], 1.0, 0.0).astype(BF)
            t = jnp.dot(one, sc, preferred_element_type=F32).astype(BF)
            out[pl.ds(o, 256), :] = t if first else out[pl.ds(o, 256), :] + t

    barrier = pltpu.get_barrier_semaphore()
    for i, to in STAGES:
        for t in i:
            pl.semaphore_signal(barrier, inc=1, device_id=to(*t), device_id_type=MESH)
    pl.semaphore_wait(barrier, len(PLANE) + len(DEPTH))
    pkm[...] = jnp.zeros_like(pkm)

    steps = (
        (pick, 0), (own, 0, 1), (pick, 2), (own, 0, 0), (load,), (pick, 1), (w1,), (r, 0, 1, 1), (f, 0, 1, 0),
        (r, 0, 1, 3), (r, 0, 0, 3), (f, 0, 0, 0), (r, 0, 0, 1), (own, 1, 0), (r, 0, 1, 2), (f, 0, 0, 1),
        (f, 1, 0, 0), (w2,), (f, 0, 1, 1), (f, 0, 1, 3), (r, 1, 0, 1), (r, 0, 0, 2), (own, 1, 1), (gu, 0, 0),
        (r, 1, 0, 3), (f, 1, 0, 1), (f, 0, 1, 2), (gu, 0, 3), (r, 1, 0, 2), (f, 1, 1, 0), (f, 0, 0, 2),
        (gu, 0, 1), (r, 1, 1, 1), (own, 2, 0), (own, 2, 1), (f, 0, 0, 3), (f, 1, 0, 3), (gu, 1, 0),
        (r, 1, 1, 3), (f, 1, 1, 1), (f, 1, 0, 2), (r, 2, 0, 1), (r, 2, 0, 3), (r, 2, 1, 1), (f, 2, 1, 0),
        (r, 2, 1, 3), (f, 1, 1, 3), (gu, 0, 2), (act, 0), (gu, 1, 1), (r, 2, 0, 2), (f, 2, 1, 1),
        (f, 2, 0, 1), (r, 1, 1, 2), (f, 2, 1, 3), (f, 2, 0, 3), (gu, 2, 0), (gu, 1, 3), (r, 2, 1, 2),
        (f, 2, 0, 2), (f, 1, 1, 2), (gu, 2, 1), (f, 2, 1, 2), (rot, 0), (f, 2, 0, 0), (by, 0), (gu, 1, 2),
        (act, 1), (gu, 2, 3), (gu, 2, 2), (act, 2), (bx, 0), (rot, 1), (by, 1), (bf, 0, 1), (bf, 0, -1),
        (rot, 2), (pks_, 0), (by, 2), (bx, 1), (pkw, 0), (pks_, 1), (bx, 2), (bf, 1, 1), (bf, 1, -1),
        (bf, 2, 1), (bf, 2, -1), (pkw, 1), (clip, 0), (d, 0, 2), (d, 0, -1), (d, 0, 0), (clip, 1), (d, 1, 2),
        (d, 1, 0), (d, 1, 1), (d, 1, -1), (clip, 2), (d, 2, 2), (d, 2, 1), (s, 1, 1), (s, 1, -1), (d, 2, 0),
        (d, 0, 1), (s, 0, 1), (s, 0, -1), (d, 2, -1), (s, 2, 1), (s, 2, -1), (fin, 1), (fin, 0), (fin, 2),
    )
    for step, *args in steps:
        step(*args)

    for c in range(NCH):
        for h in range(2):
            wait_s(xb.at[pl.ds(0, 15), rows_of(c, h)], ag_s.at[c, h])
        wait_s(hid.at[c, pl.ds(0, 240), :], a_s.at[c])
        wait_s(rout.at[c, :, pl.ds(0, 6144)], q_s.at[c])
        wait_s(cl.at[c, pl.ds(0, 3)], g_s.at[c])
        wait_s(s1.at[c], t_s.at[c, 0])
        wait_s(s2.at[c], t_s.at[c, 1])
    for i in range(3):
        wait_s(w_rows(0, 0), w1_s.at[i])
        wait_s(wd2.at[:, pl.ds(0, 384), :], w2_s.at[i])
    for i in range(2):
        wait_s(pkr.at[i, pl.ds(0, len(STAGES[i][0]))], pk_s.at[i])


def hadamard(n):
    i = jnp.arange(n, dtype=jnp.int32)
    v = i[:, None] & i[None, :]
    p = jnp.zeros_like(v)
    for b in range(n.bit_length() - 1):
        p = p ^ (v >> b & 1)
    return (1 - 2 * p).astype(BF)


def on_device(tokens, expert_ids, gate_probs, gate_weight, up_weight, down_weight):
    hits = expert_ids == 0
    routed = jnp.any(hits, axis=1)
    share = jnp.sum(jnp.where(hits, gate_probs, 0.0), axis=1)
    slot = jnp.where(routed, jnp.cumsum(routed.astype(jnp.int32)) - 1, -1)
    vm, anyspace = pl.BlockSpec(memory_space=pltpu.VMEM), pl.BlockSpec(memory_space=pl.ANY)
    V, DMA = pltpu.VMEM, pltpu.SemaphoreType.DMA
    out, peaks = pl.pallas_call(
        body,
        name="expert",
        out_shape=(jax.ShapeDtypeStruct((TOK, SL), BF), jax.ShapeDtypeStruct((8, 128), F32)),
        in_specs=[vm] * 5 + [anyspace] * 3,
        out_specs=(vm, vm),
        scratch_shapes=[
            V((16, CAP, SL), BF),
            V((4, D, 256), BF),
            V((4, 2048, SL), BF),
            V((NCH, 4, CH, 256), F32),
            V((NCH, CH, HID), BF),
            V((NCH, 16, 8192), BF),
            V((NCH, 16, 8192), BF),
            V((NCH, 4, 64, 2048), BF),
            V((NCH, CH, 2048), BF),
            V((NCH, CH, SL), BF),
            V((NCH, CH, SL), BF),
            V((NCH, 2, CH, SL), F32),
            V((NCH, CH, SL), F32),
            V((NCH, 2, CH, SL), BF),
            V((NCH, 2, CH, SL), BF),
            V((CAP, 1), F32),
            V((3, 8, 128), F32),
            V((2, 15, 8, 128), F32),
            V((8, 128), F32),
            DMA((NCH, 2, 15)), DMA((NCH, 2)),
            DMA((NCH,)), DMA((NCH,)),
            DMA((NCH, 3)), DMA((NCH,)),
            DMA((NCH, 6)), DMA((NCH,)),
            DMA((NCH, 4)), DMA((NCH, 2)),
            DMA((3,)), DMA((3,)),
            DMA((3, 3)), DMA((3,)),
            DMA((2,)), DMA((2,)),
            DMA((8,)),
        ],
        compiler_params=pltpu.CompilerParams(
            collective_id=0, has_side_effects=True, vmem_limit_bytes=66_000_000),
    )(slot[None, :], share[None, :], slot[:, None], tokens, hadamard(128), gate_weight, up_weight, down_weight)
    return out, peaks[:2, 0]


def solution(mesh):
    split = Mesh(mesh.devices.reshape(4, 4, 4, 2), (Y, X, Z, C))
    return jax.shard_map(
        on_device,
        mesh=split,
        in_specs=(P(DP, TENSOR), P(DP, None), P(DP, None), P(None, TENSOR), P(None, TENSOR), P(TENSOR, None)),
        out_specs=(P(DP, TENSOR), P()),
        check_vma=False,
    )
```

```python
import jax
import jax.numpy as jnp
from jax import lax
from jax.experimental import pallas as pl
from jax.experimental.pallas import tpu as pltpu
from jax.sharding import Mesh
from jax.sharding import PartitionSpec as P

CAP = 768
TOK = 1536
D = 6144
SL = 384
HID = 512
NCH = 3
CH = CAP // NCH
Y, X, Z, C = "tensor_0", "tensor_1", "dp_0", "dp_1"
TENSOR = (Y, X)
DP = (Z, C)
MESH = pl.DeviceIdType.MESH
clip_share = 0.25
BF, F32 = jnp.bfloat16, jnp.float32
PLANE = [(du, dv) for du in (1, -1, 2, 0) for dv in (1, -1, 2, 0) if du or dv]
DEPTH = [(dz, dc) for dz in (0, 1, -1, 2) for dc in (0, 1) if dz or dc]


def body(
    ids, probs, tok_hbm, wg, wu, wd,
    out_hbm, peaks,
    xb, wgu, wd2, acc, hid, rin, rout, cl, clp, s1, r1, pf, of, s2, r2, shs, pks, pkr, pkm, srow, scol, ex_m, tok, out, h128,
    ag_r, ag_s, a_r, a_s, q_r, q_s, g_r, g_s, t_r, t_s, w1_r, w1_s, w2_r, w2_s, pk_r, pk_s, loc,
):
    y, x, z, c_ = (lax.axis_index(a) for a in (Y, X, Z, C))
    n_ = 1 - c_
    u, v = x * n_ + y * c_, y * n_ + x * c_

    def pu(d):
        return lax.rem(u + (d + 4), 4)

    def pv(d):
        return lax.rem(v + (d + 4), 4)

    def at_uv(du, dv):
        return {Y: lax.rem(y + (du * c_ + dv * n_) + 4, 4), X: lax.rem(x + (du * n_ + dv * c_) + 4, 4)}

    def at_zc(dz, dc):
        return {Z: lax.rem(z + (dz + 4), 4), C: lax.rem(c_ + dc, 2)}

    def rcopy(src, dst, ss, rs, to):
        return pltpu.make_async_remote_copy(
            src_ref=src, dst_ref=dst, send_sem=ss, recv_sem=rs, device_id=to, device_id_type=MESH)

    def send(src, dst, ss, rs, to):
        rcopy(src, dst, ss, rs, to).start()

    def wait_s(ref, sem):
        rcopy(ref, ref, sem, pk_r.at[0], at_uv(1, 0)).wait_send()

    seen = set()

    def need(key, ref, sem):
        if key not in seen:
            seen.add(key)
            rcopy(ref, ref, pk_s.at[0], sem, at_uv(1, 0)).wait_recv()

    def mul(i, n):
        return pl.ds(pl.multiple_of(i * n, n), n)

    def tid(uu, vv):
        return (vv * 4 + uu) * n_ + (uu * 4 + vv) * c_

    def own_wd(start):
        for vv in range(4):
            k = pltpu.make_async_copy(wd.at[:, mul(tid(u, vv), SL)], wd2.at[vv, mul(u, HID), :], loc.at[4 + vv])
            k.start() if start else k.wait()

    def load():
        @pl.loop(0, 16)
        def _(s):
            src, dst = mul(tid(lax.rem(s, 4), s // 4), SL), mul(s, SL)
            for n in range(2):
                pltpu.make_async_copy(wg.at[src, pl.ds(n * 256, 256)], wgu.at[n, dst, :], loc.at[n]).start()
                pltpu.make_async_copy(wu.at[src, pl.ds(n * 256, 256)], wgu.at[2 + n, dst, :], loc.at[2 + n]).start()

        own_wd(True)

    tok_copy = pltpu.make_async_copy(tok_hbm, tok, loc.at[8])
    tok_copy.start()

    me = v * 4 + u

    def head():
        i, j = (lax.broadcasted_iota(jnp.int32, (128, 128), a) for a in (0, 1))
        both, sign = i & j, jnp.zeros((128, 128), jnp.int32)
        for b in range(7):
            sign = sign ^ (both >> b & 1)
        h128[...] = (1 - 2 * sign).astype(F32).astype(BF)
        e0, e1 = ids[pl.ds(0, 1), :] == 0, ids[pl.ds(1, 1), :] == 0
        on = jnp.where(e0 | e1, 1.0, 0.0)
        srow[pl.ds(1, 1), :] = (
            jnp.where(e0, probs[pl.ds(0, 1), :], 0.0) + jnp.where(e1, probs[pl.ds(1, 1), :], 0.0))
        on = jnp.concatenate(
            [on[:, a * 128:(a + 1) * 128] for a in range(12)] + [jnp.zeros((4, 128), F32)], axis=0)
        i, j = (lax.broadcasted_iota(jnp.int32, (128, 128), a) for a in (0, 1))
        cum = jnp.dot(on.astype(BF), jnp.where(i <= j, 1.0, 0.0).astype(BF), preferred_element_type=F32)
        tot = jnp.broadcast_to(cum[:, 127:128], (16, 128)).astype(BF)
        i, j = (lax.broadcasted_iota(jnp.int32, (16, 16), a) for a in (0, 1))
        off = jnp.dot(jnp.where(i > j, 1.0, 0.0).astype(BF), tot, preferred_element_type=F32)
        slot = jnp.where(on > 0.5, cum + off - 1.0, -1.0)
        srow[pl.ds(0, 1), :] = jnp.concatenate([slot[a:a + 1, :] for a in range(12)], axis=1)
        scol[...] = jnp.concatenate([slot, jnp.zeros((112, 128), F32)], axis=0).T

    def pick(c):
        hit = (lax.broadcasted_iota(jnp.int32, (CH, TOK), 0) + c * CH).astype(F32) == srow[pl.ds(0, 1), :]
        one = jnp.where(hit, 1.0, 0.0).astype(BF)
        if c == 0:
            tok_copy.wait()
        rows = jnp.dot(one, tok[...], preferred_element_type=F32)
        xb[me, pl.ds(c * CH, CH), :] = rows.astype(BF)
        shs[pl.ds(c * CH, CH), :] = jnp.sum(jnp.where(hit, srow[pl.ds(1, 1), :], 0.0), axis=1, keepdims=True)
        m = jnp.max(jnp.max(jnp.abs(rows), axis=0, keepdims=True), axis=1, keepdims=True)
        pkm[pl.ds(0, 1), :] = jnp.maximum(pkm[pl.ds(0, 1), :], m)

    def rows_of(c, h):
        return pl.ds(c * CH + h * 128, 128)

    def piece(c, h, ka, kb):
        du, dv = (ka, kb) if h == 0 else (kb, ka)
        return xb.at[pv(dv) * 4 + pu(du), rows_of(c, h)]

    def ag_send(c, h, ka, kb, second, d, idx):
        p = piece(c, h, ka, kb)
        along_u = (h == 0) != second
        send(p, p, ag_s.at[c, h], ag_r.at[c, h, idx], at_uv(d, 0) if along_u else at_uv(0, d))

    def ag_need(c, h, idx):
        if idx < 3:
            ka, kb = (-1, 1, 2)[idx], 0
        else:
            ka, kb = (idx - 3) // 3, (-1, 1, 2)[(idx - 3) % 3]
        need(("ag", c, h, idx), piece(c, h, ka, kb), ag_r.at[c, h, idx])

    def line(c, h, k):
        ag_send(c, h, k, 0, True, 1, 3 + 3 * k)
        ag_send(c, h, k, 0, True, -1, 4 + 3 * k)

    def own(c, h):
        ag_send(c, h, 0, 0, False, 1, 0)
        ag_send(c, h, 0, 0, False, -1, 1)
        line(c, h, 0)

    def r(c, h, k):
        forward = (c + h) % 2 == 0
        ag_need(c, h, {3: 0, 1: 1, 2: 2}[k])
        if k == 3 and forward:
            ag_send(c, h, -1, 0, False, 1, 2)
        if k == 1 and not forward:
            ag_send(c, h, 1, 0, False, -1, 2)
        line(c, h, k)

    def f(c, h, k):
        if k % 2 == 0:
            ag_need(c, h, 3 + 3 * k)
            ag_send(c, h, k, -1, True, 1, 5 + 3 * k)
        else:
            ag_need(c, h, 4 + 3 * k)
            ag_send(c, h, k, 1, True, -1, 5 + 3 * k)

    started = set()

    def gu(c, dv):
        if dv == 0:
            idxs = [(0, i) for i in (0, 1, 2)] + [(1, i) for i in (3, 4, 5)]
        else:
            e = {1: 1, 3: 0, 2: 2}[dv]
            idxs = [(0, 3 + 3 * k + e) for k in range(4)] + [(1, e)] + [(1, 3 + 3 * dv + i) for i in range(3)]
        for h, i in idxs:
            ag_need(c, h, i)
        if not started:
            for n in range(4):
                pltpu.make_async_copy(wg.at[:, pl.ds(0, 256)], wgu.at[n], loc.at[n]).wait()
        first = c not in started
        started.add(c)
        vv = pv(dv)

        @pl.loop(0, 4)
        def _(n):
            lhs = jnp.concatenate([xb[vv * 4 + uu, pl.ds(c * CH, CH), :] for uu in range(4)], axis=1)
            t = jnp.dot(lhs, wgu[n, mul(vv, 1536), :], preferred_element_type=F32)
            acc[c, n] = t if first else acc[c, n] + t

    def act(c):
        for n in range(2):
            g = acc[c, n]
            hid[c, :, pl.ds(n * 256, 256)] = (g / (1.0 + jnp.exp(-g)) * acc[c, 2 + n]).astype(BF)
        for du, dv in PLANE:
            send(hid.at[c, mul(pu(du) * 4 + pv(dv), 16), :], rin.at[c, :, mul(me, HID)],
                 a_s.at[c], a_r.at[c], at_uv(du, dv))
        rin[c, :, mul(me, HID)] = hid[c, mul(u * 4 + v, 16), :]

    def rot(c):
        need(("a", c), rin.at[c, :, pl.ds(0, 15 * HID)], a_r.at[c])
        w = jnp.concatenate([rin[c, :, pl.ds(a * 128, 128)] for a in range(64)], axis=0)
        w = jnp.dot(w, h128[...], preferred_element_type=F32)
        for s in range(6):
            n = 16 << s
            w = w.reshape(1024 // (2 * n), 2, n, 128)
            p, q = w[:, 0:1], w[:, 1:2]
            w = jnp.concatenate([p + q, p - q], axis=1)
        w = w.reshape(1024, 128) * (1.0 / 8192.0 ** 0.5)
        m = jnp.max(jnp.max(jnp.abs(w), axis=0, keepdims=True), axis=1, keepdims=True)
        pkm[pl.ds(1, 1), :] = jnp.maximum(pkm[pl.ds(1, 1), :], m)
        w = w.astype(BF)
        for a in range(64):
            rout[c, :, pl.ds(a * 128, 128)] = w[a * 16:(a + 1) * 16]

    def by(c):
        for d in (1, -1, 2):
            send(rout.at[c, :, mul(pv(d), 2048)], cl.at[c, u, mul(v, 16), :],
                 q_s.at[c], q_r.at[c, d % 4 - 1], at_uv(0, d))
        cl[c, u, mul(v, 16), :] = rout[c, :, mul(v, 2048)]

    lo32, hi32 = pl.ds(0, 32), pl.ds(32, 32)

    def by_need(c):
        for d in (1, -1, 2):
            need(("q", c, d), cl.at[c, u, mul(pv(-d), 16), :], q_r.at[c, d % 4 - 1])

    def bx(c):
        by_need(c)
        for part, d, i in ((lo32, 1, 0), (hi32, -1, 3), (hi32, 1, 1), (lo32, -1, 2)):
            p = cl.at[c, u, part, :]
            send(p, p, g_s.at[c], g_r.at[c, i], at_uv(d, 0))

    def bf(c, d):
        if d == -1:
            p = cl.at[c, pu(-1), lo32, :]
            need(("g", c, 0), p, g_r.at[c, 0])
            send(p, p, g_s.at[c], g_r.at[c, 4], at_uv(1, 0))
        else:
            p = cl.at[c, pu(1), hi32, :]
            need(("g", c, 3), p, g_r.at[c, 3])
            send(p, p, g_s.at[c], g_r.at[c, 5], at_uv(-1, 0))

    def clip(c):
        by_need(c)
        for i, (k, part) in enumerate(((-1, lo32), (-1, hi32), (1, lo32), (1, hi32), (2, lo32), (2, hi32))):
            need(("g", c, i), cl.at[c, pu(k), part, :], g_r.at[c, i])
        lim = (clip_share * pks[2, pl.ds(1, 1), pl.ds(0, 1)]).astype(BF)
        for uu in range(4):
            clp[c, pl.ds(uu * 64, 64), :] = jnp.minimum(jnp.maximum(cl[c, uu], -lim), lim)

    def w_rows(g, zz):
        return wd2.at[:, pl.ds(pl.multiple_of(g * HID + zz * 128, 128), 128), :]

    def w1():
        for d in (1, -1, 2):
            for vv in range(4):
                send(wd.at[mul(z, 128), mul(tid(pu(d), vv), SL)],
                     wd2.at[vv, pl.ds(pl.multiple_of(u * HID + z * 128, 128), 128), :],
                     w1_s.at[d % 4 - 1], w1_r.at[d % 4 - 1], at_uv(d, 0))

    def w2():
        for d in (1, -1, 2):
            need(("w1", d), w_rows(pu(-d), z), w1_r.at[d % 4 - 1])
        for dz in (1, -1, 2):
            for d in (1, -1, 2):
                p = w_rows(pu(d), z)
                send(p, p, w2_s.at[d % 4 - 1], w2_r.at[dz % 4 - 1, d % 4 - 1], at_zc(dz, 0))

    STAGES = ((DEPTH, at_zc), (PLANE, at_uv))

    def pks_(i):
        if i == 0:
            pks[0] = pkm[...]
        for j, to in enumerate(STAGES[i][0]):
            send(pks.at[i], pkr.at[i, j], pk_s.at[i], pk_r.at[i], STAGES[i][1](*to))

    def pkw(i):
        n = len(STAGES[i][0])
        need(("pk", i), pkr.at[i, pl.ds(0, n)], pk_r.at[i])
        pks[i + 1] = jnp.maximum(pks[i], jnp.max(pkr[i, pl.ds(0, n)], axis=0))
        if i == 1:
            peaks[0] = pks[2, 0, 0]
            peaks[1] = pks[2, 1, 0]

    lo, hi = pl.ds(0, 128), pl.ds(128, 128)

    def d(c, k):
        for dz in (1, -1, 2):
            for j in (1, -1, 2):
                need(("w2", dz, j), w_rows(pu(j), lax.rem(z - dz + 4, 4)), w2_r.at[dz % 4 - 1, j % 4 - 1])
        if "wd" not in seen:
            seen.add("wd")
            own_wd(False)
        t = jnp.dot(clp[c], wd2[pv(k)], preferred_element_type=F32)
        if k == 2:
            s1[c] = t.astype(BF)
            send(s1.at[c, lo, :], r1.at[c, lo, :], t_s.at[c, 0], t_r.at[c, 0], at_uv(0, -1))
            send(s1.at[c, hi, :], r1.at[c, hi, :], t_s.at[c, 0], t_r.at[c, 1], at_uv(0, 1))
        elif k == 0:
            of[c] = t
        else:
            pf[c, (k + 1) // 2] = t

    def s(c, k):
        if k == -1:
            need(("t", c, 0), r1.at[c, lo, :], t_r.at[c, 0])
            s2[c, 0, lo, :] = (pf[c, 0, lo, :] + r1[c, lo, :].astype(F32)).astype(BF)
            s2[c, 0, hi, :] = pf[c, 0, hi, :].astype(BF)
            send(s2.at[c, 0], r2.at[c, 0], t_s.at[c, 1], t_r.at[c, 2], at_uv(0, -1))
        else:
            need(("t", c, 1), r1.at[c, hi, :], t_r.at[c, 1])
            s2[c, 1, lo, :] = pf[c, 1, lo, :].astype(BF)
            s2[c, 1, hi, :] = (pf[c, 1, hi, :] + r1[c, hi, :].astype(F32)).astype(BF)
            send(s2.at[c, 1], r2.at[c, 1], t_s.at[c, 1], t_r.at[c, 3], at_uv(0, 1))

    done = set()

    def fin(c):
        need(("t", c, 2), r2.at[c, 0], t_r.at[c, 2])
        need(("t", c, 3), r2.at[c, 1], t_r.at[c, 3])
        tot = of[c] + r2[c, 0].astype(F32) + r2[c, 1].astype(F32)
        sc = (tot * shs[pl.ds(c * CH, CH), :]).astype(BF)
        first = not done
        done.add(c)
        last = len(done) == NCH

        @pl.loop(0, TOK, step=256)
        def _(o):
            o = pl.multiple_of(o, 256)
            t = jnp.dot(ex_m[c, pl.ds(o, 256), :], sc, preferred_element_type=F32).astype(BF)
            out[pl.ds(o, 256), :] = t if first else out[pl.ds(o, 256), :] + t
            if last:
                pltpu.make_async_copy(out.at[pl.ds(o, 256), :], out_hbm.at[pl.ds(o, 256), :], loc.at[9]).start()

        if last:
            pltpu.make_async_copy(out, out_hbm, loc.at[9]).wait()

    def ex(c):
        slots = (lax.broadcasted_iota(jnp.int32, (128, CH), 1) + c * CH).astype(F32)
        for a in range(12):
            ex_m[c, pl.ds(a * 128, 128), :] = jnp.where(slots == scol[:, a:a + 1], 1.0, 0.0).astype(BF)

    barrier = pltpu.get_barrier_semaphore()
    for i, to in STAGES:
        for t in i:
            pl.semaphore_signal(barrier, inc=1, device_id=to(*t), device_id_type=MESH)
    pl.semaphore_wait(barrier, len(PLANE) + len(DEPTH))
    pkm[...] = jnp.zeros_like(pkm)

    steps = (
        (head,), (pick, 0), (own, 0, 0), (w1,), (ex, 2), (ex, 0), (own, 0, 1), (load,), (ex, 1), (pick, 1),
        (r, 0, 0, 3), (f, 0, 0, 0), (pick, 2), (r, 0, 1, 3), (r, 0, 1, 1), (f, 0, 0, 3), (r, 0, 1, 2),
        (f, 0, 1, 0), (r, 0, 0, 2), (own, 1, 1), (own, 1, 0), (f, 0, 1, 3), (f, 0, 1, 1), (w2,), (f, 0, 0, 2),
        (gu, 0, 0), (r, 1, 1, 3), (r, 1, 1, 1), (f, 1, 1, 0), (r, 1, 0, 1), (f, 1, 0, 0), (r, 1, 0, 3),
        (f, 1, 1, 3), (f, 0, 1, 2), (r, 0, 0, 1), (f, 1, 0, 1), (r, 1, 1, 2), (f, 1, 1, 1), (f, 1, 0, 3),
        (r, 1, 0, 2), (own, 2, 0), (own, 2, 1), (gu, 0, 1), (f, 0, 0, 1), (gu, 1, 0), (f, 1, 1, 2),
        (gu, 0, 3), (r, 2, 0, 3), (f, 1, 0, 2), (gu, 1, 1), (gu, 1, 3), (r, 2, 0, 1), (f, 2, 0, 0),
        (f, 2, 1, 0), (r, 2, 1, 1), (r, 2, 1, 3), (gu, 0, 2), (r, 2, 0, 2), (act, 0), (f, 2, 0, 3),
        (f, 2, 0, 1), (gu, 2, 0), (f, 2, 1, 1), (gu, 1, 2), (r, 2, 1, 2), (f, 2, 1, 3), (act, 1),
        (f, 2, 0, 2), (gu, 2, 1), (f, 2, 1, 2), (rot, 0), (gu, 2, 3), (by, 0), (gu, 2, 2), (act, 2), (rot, 1),
        (by, 1), (bx, 0), (rot, 2), (pks_, 0), (by, 2), (bf, 0, 1), (bf, 0, -1), (bx, 1), (pkw, 0), (pks_, 1),
        (bx, 2), (bf, 1, 1), (bf, 1, -1), (bf, 2, 1), (bf, 2, -1), (pkw, 1), (clip, 0), (d, 0, 2), (d, 0, -1),
        (d, 0, 1), (clip, 1), (d, 1, 2), (clip, 2), (d, 2, 2), (s, 0, 1), (s, 0, -1), (d, 2, 1), (d, 1, 1),
        (d, 1, -1), (s, 1, 1), (s, 1, -1), (s, 2, 1), (d, 2, -1), (s, 2, -1), (d, 1, 0), (d, 2, 0), (d, 0, 0),
        (fin, 0), (fin, 1), (fin, 2),
    )
    for step, *args in steps:
        step(*args)

    for c in range(NCH):
        for h in range(2):
            wait_s(xb.at[pl.ds(0, 15), rows_of(c, h)], ag_s.at[c, h])
        wait_s(hid.at[c, pl.ds(0, 240), :], a_s.at[c])
        wait_s(rout.at[c, :, pl.ds(0, 6144)], q_s.at[c])
        wait_s(cl.at[c, pl.ds(0, 3)], g_s.at[c])
        wait_s(s1.at[c], t_s.at[c, 0])
        wait_s(s2.at[c], t_s.at[c, 1])
    for i in range(3):
        wait_s(w_rows(0, 0), w1_s.at[i])
        wait_s(wd2.at[:, pl.ds(0, 384), :], w2_s.at[i])
    for i in range(2):
        wait_s(pkr.at[i, pl.ds(0, len(STAGES[i][0]))], pk_s.at[i])


def on_device(tokens, expert_ids, gate_probs, gate_weight, up_weight, down_weight):
    vm, anyspace = pl.BlockSpec(memory_space=pltpu.VMEM), pl.BlockSpec(memory_space=pl.ANY)
    V, DMA = pltpu.VMEM, pltpu.SemaphoreType.DMA
    out, peaks = pl.pallas_call(
        body,
        name="expert",
        out_shape=(jax.ShapeDtypeStruct((TOK, SL), BF), jax.ShapeDtypeStruct((2,), F32)),
        in_specs=[vm] * 2 + [anyspace] * 4,
        out_specs=(anyspace, pl.BlockSpec(memory_space=pltpu.SMEM)),
        scratch_shapes=[
            V((16, CAP, SL), BF),
            V((4, D, 256), BF),
            V((4, 2048, SL), BF),
            V((NCH, 4, CH, 256), F32),
            V((NCH, CH, HID), BF),
            V((NCH, 16, 8192), BF),
            V((NCH, 16, 8192), BF),
            V((NCH, 4, 64, 2048), BF),
            V((NCH, CH, 2048), BF),
            V((NCH, CH, SL), BF),
            V((NCH, CH, SL), BF),
            V((NCH, 2, CH, SL), F32),
            V((NCH, CH, SL), F32),
            V((NCH, 2, CH, SL), BF),
            V((NCH, 2, CH, SL), BF),
            V((CAP, 1), F32),
            V((3, 8, 128), F32),
            V((2, 15, 8, 128), F32),
            V((8, 128), F32),
            V((2, TOK), F32),
            V((128, 128), F32),
            V((NCH, TOK, CH), BF),
            V((TOK, SL), BF),
            V((TOK, SL), BF),
            V((128, 128), BF),
            DMA((NCH, 2, 15)), DMA((NCH, 2)),
            DMA((NCH,)), DMA((NCH,)),
            DMA((NCH, 3)), DMA((NCH,)),
            DMA((NCH, 6)), DMA((NCH,)),
            DMA((NCH, 4)), DMA((NCH, 2)),
            DMA((3,)), DMA((3,)),
            DMA((3, 3)), DMA((3,)),
            DMA((2,)), DMA((2,)),
            DMA((10,)),
        ],
        compiler_params=pltpu.CompilerParams(
            collective_id=0, has_side_effects=True, vmem_limit_bytes=66_000_000),
    )(expert_ids.T, gate_probs.T, tokens, gate_weight, up_weight, down_weight)
    return out, peaks


def solution(mesh):
    split = Mesh(mesh.devices.reshape(4, 4, 4, 2), (Y, X, Z, C))
    return jax.shard_map(
        on_device,
        mesh=split,
        in_specs=(P(DP, TENSOR), P(DP, None), P(DP, None), P(None, TENSOR), P(None, TENSOR), P(TENSOR, None)),
        out_specs=(P(DP, TENSOR), P()),
        check_vma=False,
    )
```

```python
import jax
import jax.numpy as jnp
from jax import lax
from jax.experimental import pallas as pl
from jax.experimental.pallas import tpu as pltpu
from jax.sharding import Mesh
from jax.sharding import PartitionSpec as P

CAP = 768
TOK = 1536
D = 6144
SL = 384
HID = 512
NCH = 3
CH = CAP // NCH
Y, X, Z, C = "tensor_0", "tensor_1", "dp_0", "dp_1"
TENSOR = (Y, X)
DP = (Z, C)
MESH = pl.DeviceIdType.MESH
clip_share = 0.25
BF, F32 = jnp.bfloat16, jnp.float32
PLANE = [(du, dv) for du in (1, -1, 2, 0) for dv in (1, -1, 2, 0) if du or dv]
DEPTH = [(dz, dc) for dz in (0, 1, -1, 2) for dc in (0, 1) if dz or dc]


def body(
    ids, probs, tok_hbm, wg, wu, wd,
    out_hbm, peaks,
    xb, wgu, wd2, acc, hid, rin, rout, cl, clp, s1, r1, pf, of, s2, r2, shs, pks, pkr, pkm, srow, scol, ex_m, tok, out, h128,
    ag_r, ag_s, a_r, a_s, q_r, q_s, g_r, g_s, t_r, t_s, w1_r, w1_s, w2_r, w2_s, pk_r, pk_s, loc,
):
    y, x, z, c_ = (lax.axis_index(a) for a in (Y, X, Z, C))
    n_ = 1 - c_
    u, v = x * n_ + y * c_, y * n_ + x * c_

    def pu(d):
        return lax.rem(u + (d + 4), 4)

    def pv(d):
        return lax.rem(v + (d + 4), 4)

    def at_uv(du, dv):
        return {Y: lax.rem(y + (du * c_ + dv * n_) + 4, 4), X: lax.rem(x + (du * n_ + dv * c_) + 4, 4)}

    def at_zc(dz, dc):
        return {Z: lax.rem(z + (dz + 4), 4), C: lax.rem(c_ + dc, 2)}

    def rcopy(src, dst, ss, rs, to):
        return pltpu.make_async_remote_copy(
            src_ref=src, dst_ref=dst, send_sem=ss, recv_sem=rs, device_id=to, device_id_type=MESH)

    def send(src, dst, ss, rs, to):
        rcopy(src, dst, ss, rs, to).start()

    def wait_s(ref, sem):
        rcopy(ref, ref, sem, pk_r.at[0], at_uv(1, 0)).wait_send()

    seen = set()

    def need(key, ref, sem):
        if key not in seen:
            seen.add(key)
            rcopy(ref, ref, pk_s.at[0], sem, at_uv(1, 0)).wait_recv()

    def mul(i, n):
        return pl.ds(pl.multiple_of(i * n, n), n)

    def tid(uu, vv):
        return (vv * 4 + uu) * n_ + (uu * 4 + vv) * c_

    def own_wd(start):
        for vv in range(4):
            k = pltpu.make_async_copy(wd.at[:, mul(tid(u, vv), SL)], wd2.at[vv, mul(u, HID), :], loc.at[4 + vv])
            k.start() if start else k.wait()

    def load():
        @pl.loop(0, 16)
        def _(s):
            src, dst = mul(tid(lax.rem(s, 4), s // 4), SL), mul(s, SL)
            for n in range(2):
                pltpu.make_async_copy(wg.at[src, pl.ds(n * 256, 256)], wgu.at[n, dst, :], loc.at[n]).start()
                pltpu.make_async_copy(wu.at[src, pl.ds(n * 256, 256)], wgu.at[2 + n, dst, :], loc.at[2 + n]).start()

        own_wd(True)

    tok_copy = pltpu.make_async_copy(tok_hbm, tok, loc.at[8])
    tok_copy.start()

    barrier = pltpu.get_barrier_semaphore()
    for i, to in ((DEPTH, at_zc), (PLANE, at_uv)):
        for t in i:
            pl.semaphore_signal(barrier, inc=1, device_id=to(*t), device_id_type=MESH)

    def here():
        pl.semaphore_wait(barrier, len(PLANE) + len(DEPTH))

    me = v * 4 + u

    def head():
        pkm[...] = jnp.zeros_like(pkm)
        i, j = (lax.broadcasted_iota(jnp.int32, (128, 128), a) for a in (0, 1))
        both, sign = i & j, jnp.zeros((128, 128), jnp.int32)
        for b in range(7):
            sign = sign ^ (both >> b & 1)
        h128[...] = (1 - 2 * sign).astype(F32).astype(BF)
        e0, e1 = ids[pl.ds(0, 1), :] == 0, ids[pl.ds(1, 1), :] == 0
        on = jnp.where(e0 | e1, 1.0, 0.0)
        srow[pl.ds(1, 1), :] = (
            jnp.where(e0, probs[pl.ds(0, 1), :], 0.0) + jnp.where(e1, probs[pl.ds(1, 1), :], 0.0))
        on = jnp.concatenate(
            [on[:, a * 128:(a + 1) * 128] for a in range(12)] + [jnp.zeros((4, 128), F32)], axis=0)
        i, j = (lax.broadcasted_iota(jnp.int32, (128, 128), a) for a in (0, 1))
        cum = jnp.dot(on.astype(BF), jnp.where(i <= j, 1.0, 0.0).astype(BF), preferred_element_type=F32)
        tot = jnp.broadcast_to(cum[:, 127:128], (16, 128)).astype(BF)
        i, j = (lax.broadcasted_iota(jnp.int32, (16, 16), a) for a in (0, 1))
        off = jnp.dot(jnp.where(i > j, 1.0, 0.0).astype(BF), tot, preferred_element_type=F32)
        slot = jnp.where(on > 0.5, cum + off - 1.0, -1.0)
        srow[pl.ds(0, 1), :] = jnp.concatenate([slot[a:a + 1, :] for a in range(12)], axis=1)
        scol[...] = jnp.concatenate([slot, jnp.zeros((112, 128), F32)], axis=0).T

    def pick(c):
        hit = (lax.broadcasted_iota(jnp.int32, (CH, TOK), 0) + c * CH).astype(F32) == srow[pl.ds(0, 1), :]
        one = jnp.where(hit, 1.0, 0.0).astype(BF)
        if c == 0:
            tok_copy.wait()
        rows = jnp.dot(one, tok[...], preferred_element_type=F32)
        xb[me, pl.ds(c * CH, CH), :] = rows.astype(BF)
        shs[pl.ds(c * CH, CH), :] = jnp.sum(jnp.where(hit, srow[pl.ds(1, 1), :], 0.0), axis=1, keepdims=True)
        m = jnp.max(jnp.max(jnp.abs(rows), axis=0, keepdims=True), axis=1, keepdims=True)
        pkm[pl.ds(0, 1), :] = jnp.maximum(pkm[pl.ds(0, 1), :], m)

    def rows_of(c, h):
        return pl.ds(c * CH + h * 128, 128)

    def piece(c, h, ka, kb):
        du, dv = (ka, kb) if h == 0 else (kb, ka)
        return xb.at[pv(dv) * 4 + pu(du), rows_of(c, h)]

    def ag_send(c, h, ka, kb, second, d, idx):
        p = piece(c, h, ka, kb)
        along_u = (h == 0) != second
        send(p, p, ag_s.at[c, h], ag_r.at[c, h, idx], at_uv(d, 0) if along_u else at_uv(0, d))

    def ag_need(c, h, idx):
        if idx < 3:
            ka, kb = (-1, 1, 2)[idx], 0
        else:
            ka, kb = (idx - 3) // 3, (-1, 1, 2)[(idx - 3) % 3]
        need(("ag", c, h, idx), piece(c, h, ka, kb), ag_r.at[c, h, idx])

    def line(c, h, k):
        ag_send(c, h, k, 0, True, 1, 3 + 3 * k)
        ag_send(c, h, k, 0, True, -1, 4 + 3 * k)

    def own(c, h):
        ag_send(c, h, 0, 0, False, 1, 0)
        ag_send(c, h, 0, 0, False, -1, 1)
        line(c, h, 0)

    def r(c, h, k):
        forward = (c + h) % 2 == 0
        ag_need(c, h, {3: 0, 1: 1, 2: 2}[k])
        if k == 3 and forward:
            ag_send(c, h, -1, 0, False, 1, 2)
        if k == 1 and not forward:
            ag_send(c, h, 1, 0, False, -1, 2)
        line(c, h, k)

    def f(c, h, k):
        if k % 2 == 0:
            ag_need(c, h, 3 + 3 * k)
            ag_send(c, h, k, -1, True, 1, 5 + 3 * k)
        else:
            ag_need(c, h, 4 + 3 * k)
            ag_send(c, h, k, 1, True, -1, 5 + 3 * k)

    started = set()

    def gu(c, dv):
        if dv == 0:
            idxs = [(0, i) for i in (0, 1, 2)] + [(1, i) for i in (3, 4, 5)]
        else:
            e = {1: 1, 3: 0, 2: 2}[dv]
            idxs = [(0, 3 + 3 * k + e) for k in range(4)] + [(1, e)] + [(1, 3 + 3 * dv + i) for i in range(3)]
        for h, i in idxs:
            ag_need(c, h, i)
        if not started:
            for n in range(4):
                pltpu.make_async_copy(wg.at[:, pl.ds(0, 256)], wgu.at[n], loc.at[n]).wait()
        first = c not in started
        started.add(c)
        vv = pv(dv)

        @pl.loop(0, 4)
        def _(n):
            lhs = jnp.concatenate([xb[vv * 4 + uu, pl.ds(c * CH, CH), :] for uu in range(4)], axis=1)
            t = jnp.dot(lhs, wgu[n, mul(vv, 1536), :], preferred_element_type=F32)
            acc[c, n] = t if first else acc[c, n] + t

    def act(c):
        for n in range(2):
            g = acc[c, n]
            hid[c, :, pl.ds(n * 256, 256)] = (g / (1.0 + jnp.exp(-g)) * acc[c, 2 + n]).astype(BF)
        for du, dv in PLANE:
            send(hid.at[c, mul(pu(du) * 4 + pv(dv), 16), :], rin.at[c, :, mul(me, HID)],
                 a_s.at[c], a_r.at[c], at_uv(du, dv))
        rin[c, :, mul(me, HID)] = hid[c, mul(u * 4 + v, 16), :]

    def rot(c):
        need(("a", c), rin.at[c, :, pl.ds(0, 15 * HID)], a_r.at[c])
        w = jnp.concatenate([rin[c, :, pl.ds(a * 128, 128)] for a in range(64)], axis=0)
        w = jnp.dot(w, h128[...], preferred_element_type=F32)
        for s in range(6):
            n = 16 << s
            w = w.reshape(1024 // (2 * n), 2, n, 128)
            p, q = w[:, 0:1], w[:, 1:2]
            w = jnp.concatenate([p + q, p - q], axis=1)
        w = w.reshape(1024, 128) * (1.0 / 8192.0 ** 0.5)
        m = jnp.max(jnp.max(jnp.abs(w), axis=0, keepdims=True), axis=1, keepdims=True)
        pkm[pl.ds(1, 1), :] = jnp.maximum(pkm[pl.ds(1, 1), :], m)
        w = w.astype(BF)
        for a in range(64):
            rout[c, :, pl.ds(a * 128, 128)] = w[a * 16:(a + 1) * 16]

    def by(c):
        for d in (1, -1, 2):
            send(rout.at[c, :, mul(pv(d), 2048)], cl.at[c, u, mul(v, 16), :],
                 q_s.at[c], q_r.at[c, d % 4 - 1], at_uv(0, d))
        cl[c, u, mul(v, 16), :] = rout[c, :, mul(v, 2048)]

    lo32, hi32 = pl.ds(0, 32), pl.ds(32, 32)

    def by_need(c):
        for d in (1, -1, 2):
            need(("q", c, d), cl.at[c, u, mul(pv(-d), 16), :], q_r.at[c, d % 4 - 1])

    def bx(c):
        by_need(c)
        for part, d, i in ((lo32, 1, 0), (hi32, -1, 3), (hi32, 1, 1), (lo32, -1, 2)):
            p = cl.at[c, u, part, :]
            send(p, p, g_s.at[c], g_r.at[c, i], at_uv(d, 0))

    def bf(c, d):
        if d == -1:
            p = cl.at[c, pu(-1), lo32, :]
            need(("g", c, 0), p, g_r.at[c, 0])
            send(p, p, g_s.at[c], g_r.at[c, 4], at_uv(1, 0))
        else:
            p = cl.at[c, pu(1), hi32, :]
            need(("g", c, 3), p, g_r.at[c, 3])
            send(p, p, g_s.at[c], g_r.at[c, 5], at_uv(-1, 0))

    def clip(c):
        by_need(c)
        for i, (k, part) in enumerate(((-1, lo32), (-1, hi32), (1, lo32), (1, hi32), (2, lo32), (2, hi32))):
            need(("g", c, i), cl.at[c, pu(k), part, :], g_r.at[c, i])
        lim = (clip_share * pks[2, pl.ds(1, 1), pl.ds(0, 1)]).astype(BF)
        for uu in range(4):
            clp[c, pl.ds(uu * 64, 64), :] = jnp.minimum(jnp.maximum(cl[c, uu], -lim), lim)

    def w_rows(g, zz):
        return wd2.at[:, pl.ds(pl.multiple_of(g * HID + zz * 128, 128), 128), :]

    def w1():
        for d in (1, -1, 2):
            for vv in range(4):
                send(wd.at[mul(z, 128), mul(tid(pu(d), vv), SL)],
                     wd2.at[vv, pl.ds(pl.multiple_of(u * HID + z * 128, 128), 128), :],
                     w1_s.at[d % 4 - 1], w1_r.at[d % 4 - 1], at_uv(d, 0))

    def w2():
        for d in (1, -1, 2):
            need(("w1", d), w_rows(pu(-d), z), w1_r.at[d % 4 - 1])
        for dz in (1, -1, 2):
            for d in (1, -1, 2):
                p = w_rows(pu(d), z)
                send(p, p, w2_s.at[d % 4 - 1], w2_r.at[dz % 4 - 1, d % 4 - 1], at_zc(dz, 0))

    STAGES = ((DEPTH, at_zc), (PLANE, at_uv))

    def pks_(i):
        if i == 0:
            pks[0] = pkm[...]
        for j, to in enumerate(STAGES[i][0]):
            send(pks.at[i], pkr.at[i, j], pk_s.at[i], pk_r.at[i], STAGES[i][1](*to))

    def pkw(i):
        n = len(STAGES[i][0])
        need(("pk", i), pkr.at[i, pl.ds(0, n)], pk_r.at[i])
        pks[i + 1] = jnp.maximum(pks[i], jnp.max(pkr[i, pl.ds(0, n)], axis=0))
        if i == 1:
            peaks[0] = pks[2, 0, 0]
            peaks[1] = pks[2, 1, 0]

    lo, hi = pl.ds(0, 128), pl.ds(128, 128)

    def d(c, k):
        for dz in (1, -1, 2):
            for j in (1, -1, 2):
                need(("w2", dz, j), w_rows(pu(j), lax.rem(z - dz + 4, 4)), w2_r.at[dz % 4 - 1, j % 4 - 1])
        if "wd" not in seen:
            seen.add("wd")
            own_wd(False)
        t = jnp.dot(clp[c], wd2[pv(k)], preferred_element_type=F32)
        if k == 2:
            s1[c] = t.astype(BF)
            send(s1.at[c, lo, :], r1.at[c, lo, :], t_s.at[c, 0], t_r.at[c, 0], at_uv(0, -1))
            send(s1.at[c, hi, :], r1.at[c, hi, :], t_s.at[c, 0], t_r.at[c, 1], at_uv(0, 1))
        elif k == 0:
            of[c] = t
        else:
            pf[c, (k + 1) // 2] = t

    def s(c, k):
        if k == -1:
            need(("t", c, 0), r1.at[c, lo, :], t_r.at[c, 0])
            s2[c, 0, lo, :] = (pf[c, 0, lo, :] + r1[c, lo, :].astype(F32)).astype(BF)
            s2[c, 0, hi, :] = pf[c, 0, hi, :].astype(BF)
            send(s2.at[c, 0], r2.at[c, 0], t_s.at[c, 1], t_r.at[c, 2], at_uv(0, -1))
        else:
            need(("t", c, 1), r1.at[c, hi, :], t_r.at[c, 1])
            s2[c, 1, lo, :] = pf[c, 1, lo, :].astype(BF)
            s2[c, 1, hi, :] = (pf[c, 1, hi, :] + r1[c, hi, :].astype(F32)).astype(BF)
            send(s2.at[c, 1], r2.at[c, 1], t_s.at[c, 1], t_r.at[c, 3], at_uv(0, 1))

    done = set()

    def fin(c):
        need(("t", c, 2), r2.at[c, 0], t_r.at[c, 2])
        need(("t", c, 3), r2.at[c, 1], t_r.at[c, 3])
        tot = of[c] + r2[c, 0].astype(F32) + r2[c, 1].astype(F32)
        sc = (tot * shs[pl.ds(c * CH, CH), :]).astype(BF)
        first = not done
        done.add(c)
        last = len(done) == NCH

        @pl.loop(0, TOK, step=256)
        def _(o):
            o = pl.multiple_of(o, 256)
            t = jnp.dot(ex_m[c, pl.ds(o, 256), :], sc, preferred_element_type=F32).astype(BF)
            out[pl.ds(o, 256), :] = t if first else out[pl.ds(o, 256), :] + t
            if last:
                pltpu.make_async_copy(out.at[pl.ds(o, 256), :], out_hbm.at[pl.ds(o, 256), :], loc.at[9]).start()

        if last:
            pltpu.make_async_copy(out, out_hbm, loc.at[9]).wait()

    def ex(c):
        slots = (lax.broadcasted_iota(jnp.int32, (128, CH), 1) + c * CH).astype(F32)
        for a in range(12):
            ex_m[c, pl.ds(a * 128, 128), :] = jnp.where(slots == scol[:, a:a + 1], 1.0, 0.0).astype(BF)

    steps = (
        (head,), (pick, 0), (here,), (w1,), (own, 0, 0), (own, 0, 1), (load,), (pick, 2), (pick, 1),
        (f, 0, 0, 0), (r, 0, 1, 3), (r, 0, 1, 1), (r, 0, 1, 2), (r, 0, 0, 3), (r, 0, 0, 1), (f, 0, 1, 0),
        (f, 0, 1, 3), (w2,), (f, 0, 1, 1), (f, 0, 0, 3), (own, 1, 0), (f, 0, 1, 2), (f, 0, 0, 1), (own, 1, 1),
        (r, 0, 0, 2), (f, 1, 0, 0), (gu, 0, 0), (r, 1, 1, 3), (r, 1, 0, 3), (r, 1, 0, 1), (f, 0, 0, 2),
        (gu, 0, 3), (r, 1, 1, 1), (f, 1, 1, 0), (f, 1, 1, 3), (own, 2, 1), (gu, 0, 1), (r, 1, 1, 2),
        (r, 1, 0, 2), (f, 1, 0, 3), (own, 2, 0), (f, 1, 0, 1), (gu, 1, 0), (gu, 0, 2), (f, 2, 1, 0), (ex, 1),
        (r, 2, 1, 3), (ex, 0), (r, 2, 1, 1), (f, 1, 0, 2), (f, 1, 1, 1), (f, 1, 1, 2), (ex, 2), (r, 2, 0, 1),
        (r, 2, 0, 3), (gu, 1, 3), (f, 2, 0, 0), (f, 2, 1, 3), (f, 2, 1, 1), (r, 2, 1, 2), (act, 0),
        (gu, 1, 1), (f, 2, 0, 1), (gu, 1, 2), (f, 2, 0, 3), (r, 2, 0, 2), (gu, 2, 0), (f, 2, 1, 2),
        (f, 2, 0, 2), (act, 1), (gu, 2, 3), (gu, 2, 1), (rot, 0), (by, 0), (gu, 2, 2), (act, 2), (rot, 1),
        (by, 1), (bx, 0), (rot, 2), (by, 2), (pks_, 0), (bf, 0, -1), (bf, 0, 1), (bx, 1), (pkw, 0), (pks_, 1),
        (bx, 2), (bf, 1, 1), (bf, 1, -1), (bf, 2, -1), (bf, 2, 1), (pkw, 1), (clip, 0), (d, 0, 2), (d, 0, -1),
        (d, 0, 1), (clip, 1), (d, 1, 2), (clip, 2), (d, 2, 2), (s, 0, 1), (s, 0, -1), (d, 1, 1), (d, 2, 0),
        (d, 1, -1), (s, 1, 1), (s, 1, -1), (d, 2, 1), (s, 2, 1), (d, 2, -1), (s, 2, -1), (d, 1, 0), (d, 0, 0),
        (fin, 0), (fin, 1), (fin, 2),
    )
    for step, *args in steps:
        step(*args)

    for c in range(NCH):
        for h in range(2):
            wait_s(xb.at[pl.ds(0, 15), rows_of(c, h)], ag_s.at[c, h])
        wait_s(hid.at[c, pl.ds(0, 240), :], a_s.at[c])
        wait_s(rout.at[c, :, pl.ds(0, 6144)], q_s.at[c])
        wait_s(cl.at[c, pl.ds(0, 3)], g_s.at[c])
        wait_s(s1.at[c], t_s.at[c, 0])
        wait_s(s2.at[c], t_s.at[c, 1])
    for i in range(3):
        wait_s(w_rows(0, 0), w1_s.at[i])
        wait_s(wd2.at[:, pl.ds(0, 384), :], w2_s.at[i])
    for i in range(2):
        wait_s(pkr.at[i, pl.ds(0, len(STAGES[i][0]))], pk_s.at[i])


def on_device(tokens, expert_ids, gate_probs, gate_weight, up_weight, down_weight):
    vm, anyspace = pl.BlockSpec(memory_space=pltpu.VMEM), pl.BlockSpec(memory_space=pl.ANY)
    V, DMA = pltpu.VMEM, pltpu.SemaphoreType.DMA
    out, peaks = pl.pallas_call(
        body,
        name="expert",
        out_shape=(jax.ShapeDtypeStruct((TOK, SL), BF), jax.ShapeDtypeStruct((2,), F32)),
        in_specs=[vm] * 2 + [anyspace] * 4,
        out_specs=(anyspace, pl.BlockSpec(memory_space=pltpu.SMEM)),
        scratch_shapes=[
            V((16, CAP, SL), BF),
            V((4, D, 256), BF),
            V((4, 2048, SL), BF),
            V((NCH, 4, CH, 256), F32),
            V((NCH, CH, HID), BF),
            V((NCH, 16, 8192), BF),
            V((NCH, 16, 8192), BF),
            V((NCH, 4, 64, 2048), BF),
            V((NCH, CH, 2048), BF),
            V((NCH, CH, SL), BF),
            V((NCH, CH, SL), BF),
            V((NCH, 2, CH, SL), F32),
            V((NCH, CH, SL), F32),
            V((NCH, 2, CH, SL), BF),
            V((NCH, 2, CH, SL), BF),
            V((CAP, 1), F32),
            V((3, 8, 128), F32),
            V((2, 15, 8, 128), F32),
            V((8, 128), F32),
            V((2, TOK), F32),
            V((128, 128), F32),
            V((NCH, TOK, CH), BF),
            V((TOK, SL), BF),
            V((TOK, SL), BF),
            V((128, 128), BF),
            DMA((NCH, 2, 15)), DMA((NCH, 2)),
            DMA((NCH,)), DMA((NCH,)),
            DMA((NCH, 3)), DMA((NCH,)),
            DMA((NCH, 6)), DMA((NCH,)),
            DMA((NCH, 4)), DMA((NCH, 2)),
            DMA((3,)), DMA((3,)),
            DMA((3, 3)), DMA((3,)),
            DMA((2,)), DMA((2,)),
            DMA((10,)),
        ],
        compiler_params=pltpu.CompilerParams(
            collective_id=0, has_side_effects=True, vmem_limit_bytes=66_000_000),
    )(expert_ids.T, gate_probs.T, tokens, gate_weight, up_weight, down_weight)
    return out, peaks


def solution(mesh):
    split = Mesh(mesh.devices.reshape(4, 4, 4, 2), (Y, X, Z, C))
    return jax.shard_map(
        on_device,
        mesh=split,
        in_specs=(P(DP, TENSOR), P(DP, None), P(DP, None), P(None, TENSOR), P(None, TENSOR), P(TENSOR, None)),
        out_specs=(P(DP, TENSOR), P()),
        check_vma=False,
    )
```

```python
import jax
import jax.numpy as jnp
from jax import lax
from jax.experimental import pallas as pl
from jax.experimental.pallas import tpu as pltpu
from jax.sharding import Mesh
from jax.sharding import PartitionSpec as P

CAP = 768
TOK = 1536
D = 6144
SL = 384
HID = 512
NCH = 3
CH = CAP // NCH
Y, X, Z, C = "tensor_0", "tensor_1", "dp_0", "dp_1"
TENSOR = (Y, X)
DP = (Z, C)
MESH = pl.DeviceIdType.MESH
clip_share = 0.25
BF, F32 = jnp.bfloat16, jnp.float32
PLANE = [(du, dv) for du in (1, -1, 2, 0) for dv in (1, -1, 2, 0) if du or dv]
DEPTH = [(dz, dc) for dz in (0, 1, -1, 2) for dc in (0, 1) if dz or dc]


def body(
    ids, probs, tok_hbm, wg, wu, wd,
    out_hbm, peaks,
    xb, wgu, wd2, acc, hid, rin, rout, cl, clp, s1, r1, pf, of, s2, r2, shs, pks, pkr, pkm, srow, scol, ex_m, tok, out, h128,
    ag_r, ag_s, a_r, a_s, q_r, q_s, g_r, g_s, t_r, t_s, w1_r, w1_s, w2_r, w2_s, pk_r, pk_s, loc,
):
    y, x, z, c_ = (lax.axis_index(a) for a in (Y, X, Z, C))
    n_ = 1 - c_
    u, v = x * n_ + y * c_, y * n_ + x * c_

    def pu(d):
        return lax.rem(u + (d + 4), 4)

    def pv(d):
        return lax.rem(v + (d + 4), 4)

    def at_uv(du, dv):
        return {Y: lax.rem(y + (du * c_ + dv * n_) + 4, 4), X: lax.rem(x + (du * n_ + dv * c_) + 4, 4)}

    def at_zc(dz, dc):
        return {Z: lax.rem(z + (dz + 4), 4), C: lax.rem(c_ + dc, 2)}

    def rcopy(src, dst, ss, rs, to):
        return pltpu.make_async_remote_copy(
            src_ref=src, dst_ref=dst, send_sem=ss, recv_sem=rs, device_id=to, device_id_type=MESH)

    def send(src, dst, ss, rs, to):
        rcopy(src, dst, ss, rs, to).start()

    def wait_s(ref, sem):
        rcopy(ref, ref, sem, pk_r.at[0], at_uv(1, 0)).wait_send()

    seen = set()

    def need(key, ref, sem):
        if key not in seen:
            seen.add(key)
            rcopy(ref, ref, pk_s.at[0], sem, at_uv(1, 0)).wait_recv()

    def mul(i, n):
        return pl.ds(pl.multiple_of(i * n, n), n)

    def tid(uu, vv):
        return (vv * 4 + uu) * n_ + (uu * 4 + vv) * c_

    def own_wd(start):
        for vv in range(4):
            k = pltpu.make_async_copy(wd.at[:, mul(tid(u, vv), SL)], wd2.at[vv, mul(u, HID), :], loc.at[4 + vv])
            k.start() if start else k.wait()

    def load():
        @pl.loop(0, 16)
        def _(s):
            src, dst = mul(tid(lax.rem(s, 4), s // 4), SL), mul(s, SL)
            for n in range(2):
                pltpu.make_async_copy(wg.at[src, pl.ds(n * 256, 256)], wgu.at[n, dst, :], loc.at[n]).start()
                pltpu.make_async_copy(wu.at[src, pl.ds(n * 256, 256)], wgu.at[2 + n, dst, :], loc.at[2 + n]).start()

        own_wd(True)

    tok_copy = pltpu.make_async_copy(tok_hbm, tok, loc.at[8])
    tok_copy.start()

    barrier = pltpu.get_barrier_semaphore()
    for i, to in ((DEPTH, at_zc), (PLANE, at_uv)):
        for t in i:
            pl.semaphore_signal(barrier, inc=1, device_id=to(*t), device_id_type=MESH)

    def here():
        pl.semaphore_wait(barrier, len(PLANE) + len(DEPTH))

    me = v * 4 + u

    def head():
        pkm[...] = jnp.zeros_like(pkm)
        i, j = (lax.broadcasted_iota(jnp.int32, (128, 128), a) for a in (0, 1))
        both, sign = i & j, jnp.zeros((128, 128), jnp.int32)
        for b in range(7):
            sign = sign ^ (both >> b & 1)
        h128[...] = (1 - 2 * sign).astype(F32).astype(BF)
        e0, e1 = ids[pl.ds(0, 1), :] == 0, ids[pl.ds(1, 1), :] == 0
        on = jnp.where(e0 | e1, 1.0, 0.0)
        srow[pl.ds(1, 1), :] = (
            jnp.where(e0, probs[pl.ds(0, 1), :], 0.0) + jnp.where(e1, probs[pl.ds(1, 1), :], 0.0))
        on = jnp.concatenate(
            [on[:, a * 128:(a + 1) * 128] for a in range(12)] + [jnp.zeros((4, 128), F32)], axis=0)
        i, j = (lax.broadcasted_iota(jnp.int32, (128, 128), a) for a in (0, 1))
        cum = jnp.dot(on.astype(BF), jnp.where(i <= j, 1.0, 0.0).astype(BF), preferred_element_type=F32)
        tot = jnp.broadcast_to(cum[:, 127:128], (16, 128)).astype(BF)
        i, j = (lax.broadcasted_iota(jnp.int32, (16, 16), a) for a in (0, 1))
        off = jnp.dot(jnp.where(i > j, 1.0, 0.0).astype(BF), tot, preferred_element_type=F32)
        slot = jnp.where(on > 0.5, cum + off - 1.0, -1.0)
        srow[pl.ds(0, 1), :] = jnp.concatenate([slot[a:a + 1, :] for a in range(12)], axis=1)
        scol[...] = jnp.concatenate([slot, jnp.zeros((112, 128), F32)], axis=0).T

    def pick(c):
        hit = (lax.broadcasted_iota(jnp.int32, (CH, TOK), 0) + c * CH).astype(F32) == srow[pl.ds(0, 1), :]
        one = jnp.where(hit, 1.0, 0.0).astype(BF)
        if c == 0:
            tok_copy.wait()
        rows = jnp.dot(one, tok[...], preferred_element_type=F32)
        xb[me, pl.ds(c * CH, CH), :] = rows.astype(BF)
        shs[pl.ds(c * CH, CH), :] = jnp.sum(jnp.where(hit, srow[pl.ds(1, 1), :], 0.0), axis=1, keepdims=True)
        m = jnp.max(jnp.max(jnp.abs(rows), axis=0, keepdims=True), axis=1, keepdims=True)
        pkm[pl.ds(0, 1), :] = jnp.maximum(pkm[pl.ds(0, 1), :], m)

    def rows_of(c, h):
        return pl.ds(c * CH + h * 128, 128)

    def piece(c, h, ka, kb):
        du, dv = (ka, kb) if h == 0 else (kb, ka)
        return xb.at[pv(dv) * 4 + pu(du), rows_of(c, h)]

    def ag_send(c, h, ka, kb, second, d, idx):
        p = piece(c, h, ka, kb)
        along_u = (h == 0) != second
        send(p, p, ag_s.at[c, h], ag_r.at[c, h, idx], at_uv(d, 0) if along_u else at_uv(0, d))

    def ag_need(c, h, idx):
        if idx < 3:
            ka, kb = (-1, 1, 2)[idx], 0
        else:
            ka, kb = (idx - 3) // 3, (-1, 1, 2)[(idx - 3) % 3]
        need(("ag", c, h, idx), piece(c, h, ka, kb), ag_r.at[c, h, idx])

    def line(c, h, k):
        ag_send(c, h, k, 0, True, 1, 3 + 3 * k)
        ag_send(c, h, k, 0, True, -1, 4 + 3 * k)

    def own(c, h):
        ag_send(c, h, 0, 0, False, 1, 0)
        ag_send(c, h, 0, 0, False, -1, 1)
        line(c, h, 0)

    def r(c, h, k):
        forward = (c + h) % 2 == 0
        ag_need(c, h, {3: 0, 1: 1, 2: 2}[k])
        if k == 3 and forward:
            ag_send(c, h, -1, 0, False, 1, 2)
        if k == 1 and not forward:
            ag_send(c, h, 1, 0, False, -1, 2)
        line(c, h, k)

    def f(c, h, k):
        if k % 2 == 0:
            ag_need(c, h, 3 + 3 * k)
            ag_send(c, h, k, -1, True, 1, 5 + 3 * k)
        else:
            ag_need(c, h, 4 + 3 * k)
            ag_send(c, h, k, 1, True, -1, 5 + 3 * k)

    started = set()

    def gu(c, dv):
        if dv == 0:
            idxs = [(0, i) for i in (0, 1, 2)] + [(1, i) for i in (3, 4, 5)]
        else:
            e = {1: 1, 3: 0, 2: 2}[dv]
            idxs = [(0, 3 + 3 * k + e) for k in range(4)] + [(1, e)] + [(1, 3 + 3 * dv + i) for i in range(3)]
        for h, i in idxs:
            ag_need(c, h, i)
        if not started:
            for n in range(4):
                pltpu.make_async_copy(wg.at[:, pl.ds(0, 256)], wgu.at[n], loc.at[n]).wait()
        first = c not in started
        started.add(c)
        vv = pv(dv)

        @pl.loop(0, 4)
        def _(n):
            lhs = jnp.concatenate([xb[vv * 4 + uu, pl.ds(c * CH, CH), :] for uu in range(4)], axis=1)
            t = jnp.dot(lhs, wgu[n, mul(vv, 1536), :], preferred_element_type=F32)
            acc[c, n] = t if first else acc[c, n] + t

    def act(c):
        for n in range(2):
            g = acc[c, n]
            hid[c, :, pl.ds(n * 256, 256)] = (g / (1.0 + jnp.exp(-g)) * acc[c, 2 + n]).astype(BF)
        for du, dv in PLANE:
            send(hid.at[c, mul(pu(du) * 4 + pv(dv), 16), :], rin.at[c, :, mul(me, HID)],
                 a_s.at[c], a_r.at[c], at_uv(du, dv))
        rin[c, :, mul(me, HID)] = hid[c, mul(u * 4 + v, 16), :]

    def rot(c):
        need(("a", c), rin.at[c, :, pl.ds(0, 15 * HID)], a_r.at[c])
        w = jnp.concatenate([rin[c, :, pl.ds(a * 128, 128)] for a in range(64)], axis=0)
        w = jnp.dot(w, h128[...], preferred_element_type=F32)
        for s in range(6):
            n = 16 << s
            w = w.reshape(1024 // (2 * n), 2, n, 128)
            p, q = w[:, 0:1], w[:, 1:2]
            w = jnp.concatenate([p + q, p - q], axis=1)
        w = w.reshape(1024, 128) * (1.0 / 8192.0 ** 0.5)
        m = jnp.max(jnp.max(jnp.abs(w), axis=0, keepdims=True), axis=1, keepdims=True)
        pkm[pl.ds(1, 1), :] = jnp.maximum(pkm[pl.ds(1, 1), :], m)
        w = w.astype(BF)
        for a in range(64):
            rout[c, :, pl.ds(a * 128, 128)] = w[a * 16:(a + 1) * 16]

    def by(c):
        for d in (1, -1, 2):
            send(rout.at[c, :, mul(pv(d), 2048)], cl.at[c, u, mul(v, 16), :],
                 q_s.at[c], q_r.at[c, d % 4 - 1], at_uv(0, d))
        cl[c, u, mul(v, 16), :] = rout[c, :, mul(v, 2048)]

    lo32, hi32 = pl.ds(0, 32), pl.ds(32, 32)

    def by_need(c):
        for d in (1, -1, 2):
            need(("q", c, d), cl.at[c, u, mul(pv(-d), 16), :], q_r.at[c, d % 4 - 1])

    def bx(c):
        by_need(c)
        for part, d, i in ((lo32, 1, 0), (hi32, -1, 3), (hi32, 1, 1), (lo32, -1, 2)):
            p = cl.at[c, u, part, :]
            send(p, p, g_s.at[c], g_r.at[c, i], at_uv(d, 0))

    def bf(c, d):
        if d == -1:
            p = cl.at[c, pu(-1), lo32, :]
            need(("g", c, 0), p, g_r.at[c, 0])
            send(p, p, g_s.at[c], g_r.at[c, 4], at_uv(1, 0))
        else:
            p = cl.at[c, pu(1), hi32, :]
            need(("g", c, 3), p, g_r.at[c, 3])
            send(p, p, g_s.at[c], g_r.at[c, 5], at_uv(-1, 0))

    def clip(c):
        by_need(c)
        for i, (k, part) in enumerate(((-1, lo32), (-1, hi32), (1, lo32), (1, hi32), (2, lo32), (2, hi32))):
            need(("g", c, i), cl.at[c, pu(k), part, :], g_r.at[c, i])
        lim = (clip_share * pks[2, pl.ds(1, 1), pl.ds(0, 1)]).astype(BF)
        for uu in range(4):
            clp[c, pl.ds(uu * 64, 64), :] = jnp.minimum(jnp.maximum(cl[c, uu], -lim), lim)

    def w_rows(g, zz):
        return wd2.at[:, pl.ds(pl.multiple_of(g * HID + zz * 128, 128), 128), :]

    def w1():
        for d in (1, -1, 2):
            for vv in range(4):
                send(wd.at[mul(z, 128), mul(tid(pu(d), vv), SL)],
                     wd2.at[vv, pl.ds(pl.multiple_of(u * HID + z * 128, 128), 128), :],
                     w1_s.at[d % 4 - 1], w1_r.at[d % 4 - 1], at_uv(d, 0))

    def w2():
        for d in (1, -1, 2):
            need(("w1", d), w_rows(pu(-d), z), w1_r.at[d % 4 - 1])
        for dz in (1, -1, 2):
            for d in (1, -1, 2):
                p = w_rows(pu(d), z)
                send(p, p, w2_s.at[d % 4 - 1], w2_r.at[dz % 4 - 1, d % 4 - 1], at_zc(dz, 0))

    STAGES = ((DEPTH, at_zc), (PLANE, at_uv))

    def pks_(i):
        if i == 0:
            pks[0] = pkm[...]
        for j, to in enumerate(STAGES[i][0]):
            send(pks.at[i], pkr.at[i, j], pk_s.at[i], pk_r.at[i], STAGES[i][1](*to))

    def pkw(i):
        n = len(STAGES[i][0])
        need(("pk", i), pkr.at[i, pl.ds(0, n)], pk_r.at[i])
        pks[i + 1] = jnp.maximum(pks[i], jnp.max(pkr[i, pl.ds(0, n)], axis=0))
        if i == 1:
            peaks[0] = pks[2, 0, 0]
            peaks[1] = pks[2, 1, 0]

    lo, hi = pl.ds(0, 128), pl.ds(128, 128)

    def d(c, k):
        for dz in (1, -1, 2):
            for j in (1, -1, 2):
                need(("w2", dz, j), w_rows(pu(j), lax.rem(z - dz + 4, 4)), w2_r.at[dz % 4 - 1, j % 4 - 1])
        if "wd" not in seen:
            seen.add("wd")
            own_wd(False)
        t = jnp.dot(clp[c], wd2[pv(k)], preferred_element_type=F32)
        if k == 2:
            s1[c] = t.astype(BF)
            send(s1.at[c, lo, :], r1.at[c, lo, :], t_s.at[c, 0], t_r.at[c, 0], at_uv(0, -1))
            send(s1.at[c, hi, :], r1.at[c, hi, :], t_s.at[c, 0], t_r.at[c, 1], at_uv(0, 1))
        elif k == 0:
            of[c] = t
        else:
            side = (k + 1) // 2
            free, kept = (hi, lo) if k == -1 else (lo, hi)
            pf[c, side, kept, :] = t[:128] if k == -1 else t[128:]
            s2[c, side, free, :] = (t[128:] if k == -1 else t[:128]).astype(BF)
            send(s2.at[c, side, free, :], r2.at[c, side, free, :], t_s.at[c, 1], t_r.at[c, 4 + side], at_uv(0, k))

    def s(c, k):
        if k == -1:
            need(("t", c, 0), r1.at[c, lo, :], t_r.at[c, 0])
            s2[c, 0, lo, :] = (pf[c, 0, lo, :] + r1[c, lo, :].astype(F32)).astype(BF)
            send(s2.at[c, 0, lo, :], r2.at[c, 0, lo, :], t_s.at[c, 1], t_r.at[c, 2], at_uv(0, -1))
        else:
            need(("t", c, 1), r1.at[c, hi, :], t_r.at[c, 1])
            s2[c, 1, hi, :] = (pf[c, 1, hi, :] + r1[c, hi, :].astype(F32)).astype(BF)
            send(s2.at[c, 1, hi, :], r2.at[c, 1, hi, :], t_s.at[c, 1], t_r.at[c, 3], at_uv(0, 1))

    done = set()

    def fin(c):
        for i, side, part in ((2, 0, lo), (4, 0, hi), (3, 1, hi), (5, 1, lo)):
            need(("t", c, i), r2.at[c, side, part, :], t_r.at[c, i])
        tot = of[c] + r2[c, 0].astype(F32) + r2[c, 1].astype(F32)
        sc = (tot * shs[pl.ds(c * CH, CH), :]).astype(BF)
        first = not done
        done.add(c)
        last = len(done) == NCH

        @pl.loop(0, TOK, step=256)
        def _(o):
            o = pl.multiple_of(o, 256)
            t = jnp.dot(ex_m[c, pl.ds(o, 256), :], sc, preferred_element_type=F32).astype(BF)
            out[pl.ds(o, 256), :] = t if first else out[pl.ds(o, 256), :] + t
            if last:
                pltpu.make_async_copy(out.at[pl.ds(o, 256), :], out_hbm.at[pl.ds(o, 256), :], loc.at[9]).start()

        if last:
            pltpu.make_async_copy(out, out_hbm, loc.at[9]).wait()

    def ex(c):
        slots = (lax.broadcasted_iota(jnp.int32, (128, CH), 1) + c * CH).astype(F32)
        for a in range(12):
            ex_m[c, pl.ds(a * 128, 128), :] = jnp.where(slots == scol[:, a:a + 1], 1.0, 0.0).astype(BF)

    steps = (
        (head,), (pick, 0), (here,), (w1,), (own, 0, 0), (own, 0, 1), (load,), (pick, 2), (pick, 1),
        (f, 0, 0, 0), (r, 0, 1, 3), (r, 0, 1, 1), (r, 0, 1, 2), (r, 0, 0, 3), (r, 0, 0, 1), (f, 0, 1, 0),
        (f, 0, 1, 3), (w2,), (f, 0, 1, 1), (f, 0, 0, 3), (own, 1, 0), (f, 0, 1, 2), (f, 0, 0, 1), (own, 1, 1),
        (r, 0, 0, 2), (f, 1, 0, 0), (gu, 0, 0), (r, 1, 1, 3), (r, 1, 0, 3), (r, 1, 0, 1), (f, 0, 0, 2),
        (gu, 0, 3), (r, 1, 1, 1), (f, 1, 1, 0), (f, 1, 1, 3), (own, 2, 1), (gu, 0, 1), (r, 1, 1, 2),
        (r, 1, 0, 2), (f, 1, 0, 3), (own, 2, 0), (f, 1, 0, 1), (gu, 1, 0), (gu, 0, 2), (f, 2, 1, 0), (ex, 1),
        (r, 2, 1, 3), (ex, 0), (r, 2, 1, 1), (f, 1, 0, 2), (f, 1, 1, 1), (f, 1, 1, 2), (ex, 2), (r, 2, 0, 1),
        (r, 2, 0, 3), (gu, 1, 3), (f, 2, 0, 0), (f, 2, 1, 3), (f, 2, 1, 1), (r, 2, 1, 2), (act, 0),
        (gu, 1, 1), (f, 2, 0, 1), (gu, 1, 2), (f, 2, 0, 3), (r, 2, 0, 2), (gu, 2, 0), (f, 2, 1, 2),
        (f, 2, 0, 2), (act, 1), (gu, 2, 3), (gu, 2, 1), (rot, 0), (by, 0), (gu, 2, 2), (act, 2), (rot, 1),
        (by, 1), (bx, 0), (rot, 2), (by, 2), (pks_, 0), (bf, 0, -1), (bf, 0, 1), (bx, 1), (pkw, 0), (pks_, 1),
        (bx, 2), (bf, 1, 1), (bf, 1, -1), (bf, 2, -1), (bf, 2, 1), (pkw, 1), (clip, 0), (d, 0, 2), (d, 0, -1),
        (d, 0, 1), (clip, 1), (d, 1, 2), (clip, 2), (d, 2, 2), (s, 0, 1), (s, 0, -1), (d, 1, 1), (d, 2, 0),
        (d, 1, -1), (s, 1, 1), (s, 1, -1), (d, 2, 1), (s, 2, 1), (d, 2, -1), (s, 2, -1), (d, 1, 0), (d, 0, 0),
        (fin, 0), (fin, 1), (fin, 2),
    )
    for step, *args in steps:
        step(*args)

    for c in range(NCH):
        for h in range(2):
            wait_s(xb.at[pl.ds(0, 15), rows_of(c, h)], ag_s.at[c, h])
        wait_s(hid.at[c, pl.ds(0, 240), :], a_s.at[c])
        wait_s(rout.at[c, :, pl.ds(0, 6144)], q_s.at[c])
        wait_s(cl.at[c, pl.ds(0, 3)], g_s.at[c])
        wait_s(s1.at[c], t_s.at[c, 0])
        wait_s(s2.at[c], t_s.at[c, 1])
    for i in range(3):
        wait_s(w_rows(0, 0), w1_s.at[i])
        wait_s(wd2.at[:, pl.ds(0, 384), :], w2_s.at[i])
    for i in range(2):
        wait_s(pkr.at[i, pl.ds(0, len(STAGES[i][0]))], pk_s.at[i])


def on_device(tokens, expert_ids, gate_probs, gate_weight, up_weight, down_weight):
    vm, anyspace = pl.BlockSpec(memory_space=pltpu.VMEM), pl.BlockSpec(memory_space=pl.ANY)
    V, DMA = pltpu.VMEM, pltpu.SemaphoreType.DMA
    out, peaks = pl.pallas_call(
        body,
        name="expert",
        out_shape=(jax.ShapeDtypeStruct((TOK, SL), BF), jax.ShapeDtypeStruct((2,), F32)),
        in_specs=[vm] * 2 + [anyspace] * 4,
        out_specs=(anyspace, pl.BlockSpec(memory_space=pltpu.SMEM)),
        scratch_shapes=[
            V((16, CAP, SL), BF),
            V((4, D, 256), BF),
            V((4, 2048, SL), BF),
            V((NCH, 4, CH, 256), F32),
            V((NCH, CH, HID), BF),
            V((NCH, 16, 8192), BF),
            V((NCH, 16, 8192), BF),
            V((NCH, 4, 64, 2048), BF),
            V((NCH, CH, 2048), BF),
            V((NCH, CH, SL), BF),
            V((NCH, CH, SL), BF),
            V((NCH, 2, CH, SL), F32),
            V((NCH, CH, SL), F32),
            V((NCH, 2, CH, SL), BF),
            V((NCH, 2, CH, SL), BF),
            V((CAP, 1), F32),
            V((3, 8, 128), F32),
            V((2, 15, 8, 128), F32),
            V((8, 128), F32),
            V((2, TOK), F32),
            V((128, 128), F32),
            V((NCH, TOK, CH), BF),
            V((TOK, SL), BF),
            V((TOK, SL), BF),
            V((128, 128), BF),
            DMA((NCH, 2, 15)), DMA((NCH, 2)),
            DMA((NCH,)), DMA((NCH,)),
            DMA((NCH, 3)), DMA((NCH,)),
            DMA((NCH, 6)), DMA((NCH,)),
            DMA((NCH, 6)), DMA((NCH, 2)),
            DMA((3,)), DMA((3,)),
            DMA((3, 3)), DMA((3,)),
            DMA((2,)), DMA((2,)),
            DMA((10,)),
        ],
        compiler_params=pltpu.CompilerParams(
            collective_id=0, has_side_effects=True, vmem_limit_bytes=66_000_000),
    )(expert_ids.T, gate_probs.T, tokens, gate_weight, up_weight, down_weight)
    return out, peaks


def solution(mesh):
    split = Mesh(mesh.devices.reshape(4, 4, 4, 2), (Y, X, Z, C))
    return jax.shard_map(
        on_device,
        mesh=split,
        in_specs=(P(DP, TENSOR), P(DP, None), P(DP, None), P(None, TENSOR), P(None, TENSOR), P(TENSOR, None)),
        out_specs=(P(DP, TENSOR), P()),
        check_vma=False,
    )
```
